32 devices in a mesh: seq: 8 (over z, y), rep: 4 (over x, core).
Axes of the slice: x: 2, y: 2, z: 4, core: 2. Of those that a mesh axis runs over, the one named last changes fastest.
Arguments:
- queries: bfloat16 [4, 2048, 512], P('rep', 'seq'), may hold values from -6 to 6
- key_vectors: bfloat16 [4, 2048, 128], P('rep', 'seq'), may hold values from -6 to 6
- values: bfloat16 [4, 2048, 128], P('rep', 'seq'), may hold values from -6 to 6
- forget_logit: bfloat16 [4, 4, 2048], P('rep', None, 'seq'), may hold values from 0 to 11
- out_grad: bfloat16 [4, 2048, 512], P('rep', 'seq'), may hold values from -6 to 6
- query_gain: float32 [128], replicated, may hold values from 0.1 to 1.9
- key_gain: float32 [128], replicated, may hold values from 0.1 to 1.9
- lengths: int32 [4, 4], P('rep'), may hold values from 1 to 24, 32 in all within a row
Outputs:
- attention: bfloat16 [4, 2048, 512], P('rep', 'seq')
- query_grad: bfloat16 [4, 2048, 512], P('rep', 'seq')
- key_grad: bfloat16 [4, 2048, 128], P('rep', 'seq')
- value_grad: bfloat16 [4, 2048, 128], P('rep', 'seq')
- forget_grad: float32 [4, 4, 2048], P('rep', None, 'seq')
- norm_gain_grad: float32 [2, 128], replicated
The draws below stay inside these ranges and needn't reach their ends.
Inputs may be any that keep to these rules, and one draw needn't show every extreme that they name: `lengths`: each row lists the documents of one pack in order, in tiles of 64 tokens, and sums to 32.
All inputs are finite; a program needn't handle non-finite values.
Results may differ from the reference program's by a relative error of at most 0.02.
Values may be sent and summed in bfloat16 or wider, within the bound.
No kernel may reach another device: no remote copies, remote signals or barrier semaphores. Data moves between devices by JAX's collectives and lax.ppermute only.
A program may use at most 64 MiB of HBM per device.

```python
import math
import jax
import jax.numpy as jnp
import numpy as np
from jax import lax

QUERY_HEAD_GROUP = 4
DH = 128
TILE = 64
TILE_DEV = 4
PACK_TOTAL = 4
SERVERS = 8
TOK_DEV = 256
TOKENS_PER_PACK = 2048
TILES = 32
DOCS = 4
DOC_MOST = 24


def draw_forget_logit(key, part):
    random_split_keys = jax.random.split(key, 5)
    chain_length = DOC_MOST * TILE * 1.0
    head_keys = jax.random.split(random_split_keys[0], PACK_TOTAL)
    head_order = jax.vmap(lambda head_key: jax.random.permutation(head_key, QUERY_HEAD_GROUP))(head_keys)
    is_slow = head_order >= QUERY_HEAD_GROUP // 2
    base_rate = jnp.where(is_slow, 1.0 / chain_length, 1.0 / 40.0)[:, :, None]
    roughness = jnp.exp(jax.random.uniform(random_split_keys[1], (PACK_TOTAL, QUERY_HEAD_GROUP, TOKENS_PER_PACK), minval=-0.7, maxval=0.7))
    block_total = TOKENS_PER_PACK // TOK_DEV
    device_scale = jnp.exp(jax.random.uniform(random_split_keys[2], (PACK_TOTAL, QUERY_HEAD_GROUP, block_total, 1), minval=-0.7, maxval=0.7))
    device_scale = jnp.broadcast_to(device_scale, (PACK_TOTAL, QUERY_HEAD_GROUP, block_total, TOK_DEV)).reshape(PACK_TOTAL, QUERY_HEAD_GROUP, TOKENS_PER_PACK)
    forget_decay_rate = base_rate * roughness * device_scale
    spike_mask = jax.random.uniform(random_split_keys[3], (PACK_TOTAL, QUERY_HEAD_GROUP, TOKENS_PER_PACK)) < 6.0 / TOKENS_PER_PACK
    spike_rate = jax.random.uniform(random_split_keys[4], (PACK_TOTAL, QUERY_HEAD_GROUP, TOKENS_PER_PACK), minval=0.22, maxval=0.69)
    forget_decay_rate = jnp.where(spike_mask, spike_rate, forget_decay_rate)
    return (-jnp.log(jnp.expm1(forget_decay_rate))).astype(jnp.float32).astype(jnp.bfloat16)


def block_levels(rng, dims, cuts, least, high):
    loudness, own = 1.0, jax.random.fold_in(rng, 6)
    for axis_at, blocks in cuts:
        heights = jnp.exp(jax.random.uniform(jax.random.fold_in(own, axis_at), (blocks,), jnp.float32, least / len(cuts), high / len(cuts)))
        loudness = loudness * jnp.repeat(heights, dims[axis_at] // blocks).reshape([-1 if axis == axis_at else 1 for axis in range(len(dims))])
    return loudness


def profile(number_of, total, bound, slope):
    weights = [(1 << 20) // math.isqrt(rank ** slope) + 1 for rank in range(2, number_of + 1)]
    rest, holding = total - bound - (number_of - 1), [1] * (number_of - 1)
    while rest > 0:
        movable = [i for i in range(number_of - 1) if holding[i] < bound]
        pool, left = sum([weights[i] for i in movable]), rest
        for i in movable:
            more = min(bound - holding[i], max(1, left * weights[i] // pool), rest)
            holding[i] = holding[i] + more
            rest = rest - more
    return np.array([bound] + holding)


def ragged_sizes(key, amount, total, bound, skew):
    if amount == 2:
        one = jax.random.randint(key, (), max(1, total - bound), min(bound, total - 1) + 1)
        return jnp.stack([one, total - one])
    tallies = jnp.asarray(profile(amount, total, bound, skew), jnp.int32)
    twos = (amount - 1) // 2
    source_of, receiver = tallies[1:1 + 2 * twos:2], tallies[2:2 + 2 * twos:2]
    room = jnp.minimum(source_of - 1, bound - receiver)
    moved = jax.random.randint(jax.random.fold_in(key, 1), (twos,), 0, 1 << 20) % (room + 1)
    tallies = tallies.at[1:1 + 2 * twos:2].set(source_of - moved).at[2:2 + 2 * twos:2].set(receiver + moved)
    return tallies[jax.random.permutation(jax.random.fold_in(key, 2), amount)]


def normal_values(stream_key, shape, deviation, bound, cuts=(), kind=jnp.bfloat16):
    values = jax.random.normal(stream_key, shape, jnp.float32) * deviation
    if len(cuts) > 0:
        values = block_levels(stream_key, shape, cuts, -0.22, 0.18) * values
    return jnp.clip(values, min=-bound, max=bound).astype(kind)


def setup_inputs(seed: int = 0) -> dict:
    keys = jax.random.split(jax.random.key(seed), 9)
    queries = normal_values(keys[0], (PACK_TOTAL, TOKENS_PER_PACK, QUERY_HEAD_GROUP * DH), 1.0, 6.0, ((0, 4), (1, 8)))
    key_vectors = normal_values(keys[1], (PACK_TOTAL, TOKENS_PER_PACK, DH), 1.0, 6.0, ((0, 4), (1, 8)))
    values = normal_values(keys[2], (PACK_TOTAL, TOKENS_PER_PACK, DH), 1.0, 6.0, ((0, 4), (1, 8)))
    forget_logit = draw_forget_logit(jax.random.fold_in(keys[8], 71), 0)
    out_grad = normal_values(keys[4], (PACK_TOTAL, TOKENS_PER_PACK, QUERY_HEAD_GROUP * DH), 1.0, 6.0, ((0, 4), (1, 8)))
    query_gain = jnp.clip(1.0 + 0.18 * jax.random.normal(keys[5], (DH,), jnp.float32), 0.1, 1.9)
    key_gain = jnp.clip(1.0 + 0.18 * jax.random.normal(keys[6], (DH,), jnp.float32), 0.1, 1.9)
    lengths = jax.vmap(lambda own: ragged_sizes(own, DOCS, TILES, DOC_MOST, 2))(jax.random.split(keys[7], PACK_TOTAL)).reshape((PACK_TOTAL, DOCS)).astype(jnp.int32)
    return dict(queries=queries, key_vectors=key_vectors, values=values, forget_logit=forget_logit, out_grad=out_grad, query_gain=query_gain, key_gain=key_gain, lengths=lengths)


norm_eps = 1e-06
key_span = 512

def norm_rows(raw_values, gain_vec, factor):
    lifted = raw_values.astype(jnp.float32)
    mean_square = lax.optimization_barrier(jnp.mean(lifted * lifted, axis=-1, keepdims=True))
    return lifted * lax.rsqrt(mean_square + norm_eps) * (gain_vec * factor)

def tile_starts(lengths_row, tile_count):
    doc_ends = jnp.cumsum(lengths_row).astype(jnp.int32)
    tile_index = jnp.arange(tile_count, dtype=jnp.int32)
    passed = doc_ends[None, :] <= tile_index[:, None]
    return lax.optimization_barrier(jnp.sum(jnp.where(passed, lengths_row[None, :], 0), axis=1)).astype(jnp.int32)

def pad_rows(array_in, along):
    widths = [(0, 0)] * array_in.ndim
    widths[along] = (0, key_span)
    return jnp.pad(array_in, widths)

def block_scores(query_rows, key_pad, gate_pad, query_gate, block_first, tile_first, doc_first, head_count):
    key_block = lax.dynamic_slice_in_dim(key_pad, block_first, key_span, 0)
    scores = jnp.dot(query_rows, key_block.T, preferred_element_type=jnp.float32)
    row_count = query_rows.shape[0] // head_count
    scores = scores.reshape(head_count, row_count, key_span)
    key_gate = lax.dynamic_slice_in_dim(gate_pad, block_first, key_span, 1)
    scores = scores + query_gate[:, :, None] - key_gate[:, None, :]
    key_place = block_first + jnp.arange(key_span, dtype=jnp.int32)
    query_place = tile_first + jnp.arange(row_count, dtype=jnp.int32)
    allowed = (key_place[None, :] >= doc_first) & (key_place[None, :] <= query_place[:, None])
    return (jnp.where(allowed[None, :, :], scores, -jnp.inf), key_block)

def query_setup(query_tile, tile_id, doc_tile, gate_pad, query_gain, head_count, head_dim):
    row_count = query_tile.shape[0]
    scale_factor = head_dim ** (-0.5)
    normed = norm_rows(query_tile.reshape(row_count, head_count, head_dim), query_gain, scale_factor).astype(jnp.bfloat16)
    query_rows = normed.transpose(1, 0, 2).reshape(head_count * row_count, head_dim)
    tile_first = tile_id * row_count
    doc_first = doc_tile * row_count
    query_gate = lax.dynamic_slice_in_dim(gate_pad, tile_first, row_count, 1)
    block_count = (tile_first + row_count - doc_first + key_span - 1) // key_span
    return (query_rows, tile_first, doc_first, query_gate, block_count)

def forward_task(query_tile, tile_id, doc_tile, key_pad, value_pad, gate_pad, query_gain, head_count):
    row_count, full_width = query_tile.shape
    head_dim = key_pad.shape[1]
    query_rows, tile_first, doc_first, query_gate, block_count = query_setup(query_tile, tile_id, doc_tile, gate_pad, query_gain, head_count, head_dim)

    def block_step(block_index, loop_state):
        row_total, value_sum = loop_state
        block_first = doc_first + block_index * key_span
        scores, key_block = block_scores(query_rows, key_pad, gate_pad, query_gate, block_first, tile_first, doc_first, head_count)
        weights = jnp.exp(scores)
        value_block = lax.dynamic_slice_in_dim(value_pad, block_first, key_span, 0)
        mixed_rows = jnp.dot(weights.reshape(head_count * row_count, key_span).astype(jnp.bfloat16), value_block, preferred_element_type=jnp.float32)
        return (row_total + lax.optimization_barrier(jnp.sum(weights, axis=2)), value_sum + mixed_rows)
    start_state = (jnp.zeros((head_count, row_count), jnp.float32), jnp.zeros((head_count * row_count, head_dim), jnp.float32))
    row_total, value_sum = lax.fori_loop(0, block_count, block_step, start_state)
    result = value_sum.reshape(head_count, row_count, head_dim) / row_total[:, :, None]
    return result.transpose(1, 0, 2).reshape(row_count, full_width).astype(jnp.bfloat16)

def backward_task(partials, query_tile, grad_tile, out_tile, tile_id, doc_tile, key_pad, value_pad, gate_pad, query_gain, head_count):
    row_count, full_width = query_tile.shape
    head_dim = key_pad.shape[1]
    query_rows, tile_first, doc_first, query_gate, block_count = query_setup(query_tile, tile_id, doc_tile, gate_pad, query_gain, head_count, head_dim)
    grad_rows = grad_tile.reshape(row_count, head_count, head_dim).transpose(1, 0, 2).reshape(head_count * row_count, head_dim)
    product = grad_tile.astype(jnp.float32) * out_tile.astype(jnp.float32)
    out_inner = lax.optimization_barrier(jnp.sum(product.reshape(row_count, head_count, head_dim), axis=2)).T

    def total_step(block_index, row_total):
        block_first = doc_first + block_index * key_span
        scores, key_block = block_scores(query_rows, key_pad, gate_pad, query_gate, block_first, tile_first, doc_first, head_count)
        return row_total + lax.optimization_barrier(jnp.sum(jnp.exp(scores), axis=2))
    row_total = lax.fori_loop(0, block_count, total_step, jnp.zeros((head_count, row_count), jnp.float32))

    def grad_step(block_index, loop_state):
        key_part, value_part, gate_part, query_grad, row_sum = loop_state
        block_first = doc_first + block_index * key_span
        scores, key_block = block_scores(query_rows, key_pad, gate_pad, query_gate, block_first, tile_first, doc_first, head_count)
        probability = jnp.exp(scores) / row_total[:, :, None]
        value_block = lax.dynamic_slice_in_dim(value_pad, block_first, key_span, 0)
        prob_grad = jnp.dot(grad_rows, value_block.T, preferred_element_type=jnp.float32).reshape(head_count, row_count, key_span)
        score_grad = probability * (prob_grad - out_inner[:, :, None])
        score_low = score_grad.reshape(head_count * row_count, key_span).astype(jnp.bfloat16)
        prob_low = probability.reshape(head_count * row_count, key_span).astype(jnp.bfloat16)
        query_grad = query_grad + jnp.dot(score_low, key_block, preferred_element_type=jnp.float32)
        key_update = jnp.dot(score_low.T, query_rows, preferred_element_type=jnp.float32)
        value_update = jnp.dot(prob_low.T, grad_rows, preferred_element_type=jnp.float32)
        key_part = lax.dynamic_update_slice_in_dim(key_part, lax.dynamic_slice_in_dim(key_part, block_first, key_span, 0) + key_update, block_first, 0)
        value_part = lax.dynamic_update_slice_in_dim(value_part, lax.dynamic_slice_in_dim(value_part, block_first, key_span, 0) + value_update, block_first, 0)
        column_sum = lax.optimization_barrier(jnp.sum(score_grad, axis=1))
        gate_part = lax.dynamic_update_slice_in_dim(gate_part, lax.dynamic_slice_in_dim(gate_part, block_first, key_span, 1) - column_sum, block_first, 1)
        return (key_part, value_part, gate_part, query_grad, row_sum + lax.optimization_barrier(jnp.sum(score_grad, axis=2)))
    start_state = (partials[0], partials[1], partials[2], jnp.zeros((head_count * row_count, head_dim), jnp.float32), jnp.zeros((head_count, row_count), jnp.float32))
    key_part, value_part, gate_part, query_grad, row_sum = lax.fori_loop(0, block_count, grad_step, start_state)
    gate_part = lax.dynamic_update_slice_in_dim(gate_part, lax.dynamic_slice_in_dim(gate_part, tile_first, row_count, 1) + row_sum, tile_first, 1)
    query_result = query_grad.reshape(head_count, row_count, head_dim).transpose(1, 0, 2).reshape(row_count, full_width).astype(jnp.bfloat16)
    return ((key_part, value_part, gate_part), query_result)

def one_pack(query_local, key_local, value_local, logit_local, grad_local, query_gain, key_gain, lengths_row):
    token_count, full_width = query_local.shape
    head_dim = key_local.shape[1]
    head_count = full_width // head_dim
    tile_count = token_count // TILE
    key_normed = norm_rows(key_local, key_gain, 1.0).astype(jnp.bfloat16)
    gate = jnp.cumsum(jax.nn.log_sigmoid(logit_local.astype(jnp.float32)), axis=1)
    key_pad = pad_rows(key_normed, 0)
    value_pad = pad_rows(value_local, 0)
    gate_pad = pad_rows(gate, 1)
    starts = tile_starts(lengths_row, tile_count)
    tile_ids = jnp.arange(tile_count, dtype=jnp.int32)
    query_tiles = query_local.reshape(tile_count, TILE, full_width)
    grad_tiles = grad_local.reshape(tile_count, TILE, full_width)
    out_tiles = lax.map(lambda task_item: forward_task(task_item[0], task_item[1], task_item[2], key_pad, value_pad, gate_pad, query_gain, head_count), (query_tiles, tile_ids, starts))

    def owner_step(totals, owner_items):
        query_own, grad_own, out_own, id_own = owner_items
        zero_parts = (jnp.zeros(key_pad.shape, jnp.float32), jnp.zeros(value_pad.shape, jnp.float32), jnp.zeros(gate_pad.shape, jnp.float32))

        def task_step(partials, task_item):
            query_tile, grad_tile, out_tile, tile_id = task_item
            return backward_task(partials, query_tile, grad_tile, out_tile, tile_id, starts[tile_id], key_pad, value_pad, gate_pad, query_gain, head_count)
        partials, query_own_grad = lax.scan(task_step, zero_parts, (query_own, grad_own, out_own, id_own))
        key_part, value_part, gate_part = partials
        suffix = jnp.flip(jnp.cumsum(jnp.flip(gate_part[:, :token_count], 1), axis=1), 1)
        rounded = lax.optimization_barrier((key_part[:token_count].astype(jnp.bfloat16), value_part[:token_count].astype(jnp.bfloat16), suffix.astype(jnp.bfloat16)))
        totals = (totals[0] + rounded[0].astype(jnp.float32), totals[1] + rounded[1].astype(jnp.float32), totals[2] + rounded[2].astype(jnp.float32))
        return (totals, query_own_grad)
    zero_totals = (jnp.zeros((token_count, head_dim), jnp.float32), jnp.zeros((token_count, head_dim), jnp.float32), jnp.zeros((head_count, token_count), jnp.float32))
    grouped = (query_tiles.reshape(SERVERS, TILE_DEV, TILE, full_width), grad_tiles.reshape(SERVERS, TILE_DEV, TILE, full_width), out_tiles.reshape(SERVERS, TILE_DEV, TILE, full_width), tile_ids.reshape(SERVERS, TILE_DEV))
    totals, query_grad_tiles = lax.scan(owner_step, zero_totals, grouped)
    normed_key_grad, value_sum, gate_grad = totals
    _, key_pullback = jax.vjp(lambda raw_values, gain_vec: norm_rows(raw_values, gain_vec, 1.0), key_local.astype(jnp.float32), key_gain)
    key_input_grad, key_gain_part = key_pullback(normed_key_grad)
    scale_factor = head_dim ** (-0.5)
    _, query_pullback = jax.vjp(lambda raw_values, gain_vec: norm_rows(raw_values, gain_vec, scale_factor), query_local.reshape(token_count, head_count, head_dim).astype(jnp.float32), query_gain)
    query_input_grad, query_gain_part = query_pullback(query_grad_tiles.reshape(token_count, head_count, head_dim).astype(jnp.float32))
    forget_grad = gate_grad * jax.nn.sigmoid(-logit_local.astype(jnp.float32))
    attention = out_tiles.reshape(token_count, full_width)
    return (attention, query_input_grad.reshape(token_count, full_width).astype(jnp.bfloat16), key_input_grad.astype(jnp.bfloat16), value_sum.astype(jnp.bfloat16), forget_grad, jnp.stack([query_gain_part, key_gain_part]))

def reference(queries, key_vectors, values, forget_logit, out_grad, query_gain, key_gain, lengths):
    results = []
    for replica in range(PACK_TOTAL):
        results.append(one_pack(queries[replica], key_vectors[replica], values[replica], forget_logit[replica], out_grad[replica], query_gain, key_gain, lengths[replica]))
    attention = jnp.stack([entry[0] for entry in results])
    query_grad = jnp.stack([entry[1] for entry in results])
    key_grad = jnp.stack([entry[2] for entry in results])
    value_grad = jnp.stack([entry[3] for entry in results])
    forget_grad = jnp.stack([entry[4] for entry in results])
    norm_gain_grad = results[0][5]
    for replica in range(1, PACK_TOTAL):
        norm_gain_grad = norm_gain_grad + results[replica][5]
    return (attention, query_grad, key_grad, value_grad, forget_grad, norm_gain_grad)
```

```python
import functools

import jax
import jax.numpy as jnp
from jax import lax
from jax.experimental import pallas as pl
from jax.experimental.pallas import tpu as pltpu
from jax.sharding import PartitionSpec as P

TILE = 64
EPS = 1e-06
TAIL = 16
BIG = 1e30
F32 = jnp.float32
BF16 = jnp.bfloat16


def swap(value, axis, bit):
    count = lax.axis_size(axis)
    return lax.ppermute(value, axis, [(i, i ^ bit) for i in range(count)])


def dot_nn(a, b):
    return lax.dot_general(a, b, (((1,), (0,)), ((), ())), preferred_element_type=F32)


def dot_nt(a, b):
    return lax.dot_general(a, b, (((1,), (1,)), ((), ())), preferred_element_type=F32)


def split3(x):
    hi = x.astype(BF16).astype(F32)
    rest = x - hi
    mid = rest.astype(BF16).astype(F32)
    return hi, mid, rest - mid


def pick3(index, parts):
    return jnp.where(index == 0, parts[0], jnp.where(index == 1, parts[1], parts[2]))


def tile_rows(rows, count):
    step = rows.shape[0]
    return jnp.concatenate([rows] * (count // step), axis=0)


def attend_kernel(
    n, heads, dim, docs, *refs
):
    len_ref, q_ref, g_ref, qgain_ref, kgain_ref = refs[:5]
    raw_refs = refs[5 : 5 + n]
    out_ref, qgrad_ref, piece_ref = refs[5 + n : 8 + n]
    (raw, kaug, vaug, khat, wsc, qaug, doaug, acc, dssc, gsc, sem) = refs[8 + n :]
    rows = q_ref.shape[0]
    tiles = rows // TILE
    total_rows = heads * rows
    scale = dim ** (-0.5)
    me = lax.axis_index("seq")
    ga, ka, da = 0, 3 * heads, 3 * heads + 3

    for k in range(n):
        pltpu.make_async_copy(raw_refs[k], raw.at[k], sem.at[k]).start()

    lane1 = lax.broadcasted_iota(jnp.int32, (1, dim), 1)
    doc_lo = jnp.full((1, dim), 1, jnp.int32)
    doc_hi = jnp.zeros((1, dim), jnp.int32)
    first = me * tiles
    start = jnp.int32(0)
    begin = jnp.int32(0)
    for d in range(docs):
        finish = start + len_ref[0, d]
        doc_lo = jnp.where(lane1 == da + d, start, doc_lo)
        doc_hi = jnp.where(lane1 == da + d, finish, doc_hi)
        begin = jnp.where(start <= first, start, begin)
        start = finish
    low = begin // tiles

    lane = lax.broadcasted_iota(jnp.int32, (rows, dim), 1)
    sub = lax.broadcasted_iota(jnp.int32, (rows, dim), 0)
    lane_part = (lane - ga) // heads
    sub_tile = sub // TILE
    r_ext = lax.broadcasted_iota(jnp.int32, (rows + TAIL, rows), 0)
    c_ext = lax.broadcasted_iota(jnp.int32, (rows + TAIL, rows), 1)
    after = jnp.where((c_ext > r_ext) | (r_ext >= rows), 1.0, 0.0).astype(BF16)
    r_sq = lax.broadcasted_iota(jnp.int32, (rows, rows), 0)
    c_sq = lax.broadcasted_iota(jnp.int32, (rows, rows), 1)
    upto = jnp.where(c_sq <= r_sq, 1.0, 0.0).astype(BF16)

    def gates(k, matrix):
        tail = raw[k, rows : rows + TAIL, :].astype(F32)
        result = None
        for s in range(3):
            part = tile_rows(tail[s * heads : (s + 1) * heads], dim).astype(BF16)
            term = dot_nt(matrix, part)
            result = term if result is None else result + term
        return result

    def fill_block(k, b, key_term):
        key = raw[k, :rows, :dim].astype(F32)
        hat = key * lax.rsqrt(jnp.mean(key * key, axis=-1, keepdims=True) + EPS)
        khat[b] = hat
        kaug[b, :, :dim] = (hat * kgain_ref[...]).astype(BF16)
        extra = pick3(lane_part, split3(key_term))
        place = sub_tile + b * tiles
        inside = jnp.where((place >= doc_lo) & (place < doc_hi), 1.0, 0.0)
        extra = jnp.where(lane < ka, extra, jnp.where(lane < da, 1.0, inside))
        kaug[b, :, dim:] = extra.astype(BF16)
        vaug[b, :, :dim] = raw[k, :rows, dim:]
        vaug[b, :, dim:] = jnp.where(lane < 3, 1.0, 0.0).astype(BF16)

    def rows_of(h):
        return slice(h * rows, (h + 1) * rows)

    def cols_of(h):
        return slice(h * dim, (h + 1) * dim)

    def query_hat(h):
        x = q_ref[:, cols_of(h)].astype(F32)
        rstd = lax.rsqrt(jnp.mean(x * x, axis=-1, keepdims=True) + EPS)
        return x, rstd

    ones_rows = jnp.where(
        lax.broadcasted_iota(jnp.int32, (TAIL, rows), 0) == 0, 1.0, 0.0
    ).astype(BF16)

    def with_ones(block):
        return jnp.concatenate([block.astype(F32).T.astype(BF16), ones_rows], axis=0)

    def forward_block(b, diagonal):
        value_t = with_ones(vaug[b, :, :dim])
        for h in range(heads):
            scores = dot_nt(kaug[b], qaug[rows_of(h), :])
            if diagonal:
                scores = jnp.where(r_sq <= c_sq, scores, -BIG)
            weights = jnp.exp(scores).astype(BF16)
            wsc[b, :, rows_of(h)] = weights
            mixed = dot_nn(value_t, weights)
            if diagonal:
                acc[:, rows_of(h)] = mixed
            else:
                acc[:, rows_of(h)] += mixed

    pltpu.make_async_copy(raw_refs[0], raw.at[0], sem.at[0]).wait()
    own_gate = gates(0, upto)
    fill_block(0, me, -own_gate)
    place = sub_tile + me * tiles
    same = (place >= doc_lo) & (place < doc_hi)
    doc_term = jnp.where((lane >= da) & (lane < da + docs) & ~same, -BIG, 0.0)
    for h in range(heads):
        x, rstd = query_hat(h)
        qaug[rows_of(h), :dim] = (x * rstd * (qgain_ref[...] * scale)).astype(BF16)
        column = jnp.broadcast_to(own_gate[:, h : h + 1], (rows, dim))
        extra = pick3(lane - ka, split3(column))
        head_one = jnp.where(lane - lane_part * heads == h, 1.0, 0.0)
        extra = jnp.where(lane < ka, head_one, jnp.where(lane < da, extra, doc_term))
        qaug[rows_of(h), dim:] = extra.astype(BF16)
    forward_block(me, True)
    for k in range(1, n):
        pltpu.make_async_copy(raw_refs[k], raw.at[k], sem.at[k]).wait()

    def forward_step(t, between):
        b = me - 1 - t
        ext = gates(me ^ b, after)
        fill_block(me ^ b, b, ext[:rows] + between)
        forward_block(b, False)
        return between + ext[rows : rows + 1]

    lax.fori_loop(0, me - low, forward_step, jnp.zeros((1, dim), F32))

    for h in range(heads):
        total = acc[dim : dim + 1, rows_of(h)]
        inverse = 1.0 / total
        mixed = (acc[:dim, rows_of(h)] * inverse).T.astype(BF16)
        out_ref[:, cols_of(h)] = mixed
        inv = jnp.broadcast_to(inverse, (dim, rows)).T
        grad = g_ref[:, cols_of(h)].astype(F32)
        inner = jnp.sum(grad * mixed.astype(F32), axis=-1, keepdims=True)
        doaug[rows_of(h), :dim] = (grad * inv).astype(BF16)
        extra = pick3(lane, split3(-inner * inv))
        doaug[rows_of(h), dim:] = jnp.where(lane < 3, extra, 0.0).astype(BF16)

    later = jnp.where(r_sq >= c_sq, 1.0, 0.0).astype(BF16)

    def backward_block(b, diagonal, carry):
        key_gain, gate_sum = carry
        key_t = with_ones(kaug[b, :, :dim])
        for h in range(heads):
            prob_grad = dot_nt(vaug[b], doaug[rows_of(h), :])
            score_low = (wsc[b, :, rows_of(h)].astype(F32) * prob_grad).astype(BF16)
            dssc[:, rows_of(h)] = score_low
            back = dot_nn(key_t, score_low)
            if diagonal:
                acc[:, rows_of(h)] = back
            else:
                acc[:, rows_of(h)] += back
        key_part = dot_nn(dssc[...], qaug[...])
        value_part = dot_nn(wsc[b], doaug[...])
        k = me ^ b
        piece_ref[k, :rows, :dim] = key_part[:, :dim].astype(BF16)
        piece_ref[k, :rows, dim:] = value_part[:, :dim].astype(BF16)
        prod = key_part[:, :dim] * khat[b]
        key_gain = key_gain + jnp.sum(prod, axis=0, keepdims=True)
        columns = -(key_part[:, dim:].T)[:8]
        gsc[b] = columns
        return key_gain, gate_sum

    def backward_step(t, carry):
        return backward_block(me - 1 - t, False, carry)

    carry = (jnp.zeros((1, dim), F32), jnp.zeros((8, rows), F32))
    carry = backward_block(me, True, carry)
    key_gain, _ = lax.fori_loop(0, me - low, backward_step, carry)

    query_gain = jnp.zeros((1, dim), F32)
    row_sums = []
    for h in range(heads):
        x, rstd = query_hat(h)
        hat = x * rstd
        back = acc[:dim, rows_of(h)].T.astype(BF16).astype(F32)
        row_sums.append(acc[dim : dim + 1, rows_of(h)])
        query_gain = query_gain + jnp.sum(back * hat, axis=0, keepdims=True)
        back = back * (qgain_ref[...] * scale)
        mean = jnp.mean(back * hat, axis=-1, keepdims=True)
        qgrad_ref[:, cols_of(h)] = (rstd * (back - hat * mean)).astype(BF16)
    query_gain = query_gain * scale
    row_sum = jnp.concatenate(row_sums + row_sums, axis=0)[:8]
    gsc[me] += row_sum

    gain_row = jnp.concatenate([query_gain, key_gain], axis=1)
    g_hi, g_mid, g_lo = split3(gain_row)
    sub_tail = lax.broadcasted_iota(jnp.int32, (8, rows), 0)
    gain_rows = jnp.where(
        sub_tail == 0, g_hi, jnp.where(sub_tail == 1, g_mid, jnp.where(sub_tail == 2, g_lo, 0.0))
    )

    def gate_step(t, gate_sum):
        b = me - t
        parts = split3(gsc[b])
        suffix = gate_sum
        for part in parts:
            suffix = suffix + dot_nn(part.astype(BF16), later)
        tail = jnp.concatenate([suffix, gain_rows], axis=0)
        piece_ref[me ^ b, rows : rows + TAIL, :] = tail.astype(BF16)
        return jnp.broadcast_to(suffix[:, :1], (8, rows))

    lax.fori_loop(0, me - low + 1, gate_step, jnp.zeros((8, rows), F32))
    idle = jnp.concatenate([jnp.zeros((8, rows), F32), gain_rows], axis=0).astype(BF16)
    for k in range(1, n):
        b = me ^ k

        @pl.when((b > me) | (b < low))
        def _():
            piece_ref[k, :rows, :] = jnp.zeros((rows, 2 * dim), BF16)
            piece_ref[k, rows : rows + TAIL, :] = idle


def attend(lengths, queries, grads, query_gain, key_gain, blocks):
    n = len(blocks)
    rows, full = queries.shape
    dim = query_gain.shape[1]
    heads = full // dim
    docs = lengths.shape[1]
    vmem = pl.BlockSpec(memory_space=pltpu.VMEM)
    width = 2 * dim
    return pl.pallas_call(
        functools.partial(attend_kernel, n, heads, dim, docs),
        out_shape=(
            jax.ShapeDtypeStruct((rows, full), BF16),
            jax.ShapeDtypeStruct((rows, full), BF16),
            jax.ShapeDtypeStruct((n, rows + TAIL, width), BF16),
        ),
        in_specs=[pl.BlockSpec(memory_space=pltpu.SMEM)]
        + [vmem] * 4
        + [pl.BlockSpec(memory_space=pl.ANY)] * n,
        out_specs=(vmem, vmem, vmem),
        scratch_shapes=[
            pltpu.VMEM((n, rows + TAIL, width), BF16),
            pltpu.VMEM((n, rows, width), BF16),
            pltpu.VMEM((n, rows, width), BF16),
            pltpu.VMEM((n, rows, dim), F32),
            pltpu.VMEM((n, rows, heads * rows), BF16),
            pltpu.VMEM((heads * rows, width), BF16),
            pltpu.VMEM((heads * rows, width), BF16),
            pltpu.VMEM((dim + TAIL, heads * rows), F32),
            pltpu.VMEM((rows, heads * rows), BF16),
            pltpu.VMEM((n, 8, rows), F32),
            pltpu.SemaphoreType.DMA((n,)),
        ],
        name="attend",
    )(lengths, queries, grads, query_gain, key_gain, *blocks)


def finish_kernel(count, heads, *refs):
    k_ref, logit_ref, gain_ref = refs[:3]
    piece_refs = refs[3 : 3 + count]
    kgrad_ref, vgrad_ref, fgrad_ref, gains_ref = refs[3 + count :]
    rows, dim = k_ref.shape
    total = piece_refs[0][...].astype(F32)
    for ref in piece_refs[1:]:
        total = total + ref[...].astype(F32)
    vgrad_ref[...] = total[:rows, dim:].astype(BF16)
    x = k_ref[...].astype(F32)
    rstd = lax.rsqrt(jnp.mean(x * x, axis=-1, keepdims=True) + EPS)
    hat = x * rstd
    back = total[:rows, :dim] * gain_ref[...]
    mean = jnp.mean(back * hat, axis=-1, keepdims=True)
    kgrad_ref[...] = (rstd * (back - hat * mean)).astype(BF16)
    logit = logit_ref[...].astype(F32)
    fgrad_ref[...] = total[rows : rows + heads] * (1.0 / (1.0 + jnp.exp(logit)))
    gain = jnp.sum(total[rows + 8 : rows + TAIL], axis=0, keepdims=True)
    gains_ref[...] = jnp.concatenate([gain[:, :dim], gain[:, dim:]], axis=0)


def finish(key, logit, gain, pieces, heads):
    rows, dim = key.shape
    vmem = pl.BlockSpec(memory_space=pltpu.VMEM)
    return pl.pallas_call(
        functools.partial(finish_kernel, len(pieces), heads),
        out_shape=(
            jax.ShapeDtypeStruct((rows, dim), BF16),
            jax.ShapeDtypeStruct((rows, dim), BF16),
            jax.ShapeDtypeStruct((heads, rows), F32),
            jax.ShapeDtypeStruct((2, dim), F32),
        ),
        in_specs=[vmem] * (3 + len(pieces)),
        out_specs=(vmem,) * 4,
        name="finish",
    )(key, logit, gain, *pieces)


def payload(key, value, logit):
    heads, rows = logit.shape
    log_gate = jax.nn.log_sigmoid(logit.astype(F32))
    hi = lax.reduce_precision(log_gate, 8, 7)
    rest = log_gate - hi
    mid = lax.reduce_precision(rest, 8, 7)
    low = rest - mid
    pad = jnp.zeros((TAIL - 3 * heads, rows), F32)
    tail = jnp.concatenate([hi, mid, low, pad], axis=0).astype(BF16)
    return jnp.concatenate([jnp.concatenate([key, value], axis=1), tail], axis=0)


def on_device(queries, key_vectors, values, forget_logit, out_grad, query_gain, key_gain, lengths):
    n = lax.axis_size("seq")
    full = queries.shape[2]
    dim = query_gain.shape[0]
    heads = full // dim
    own = payload(key_vectors[0], values[0], forget_logit[0])
    blocks = {0: own}
    for k in range(n - 2, 0, -2):
        blocks[k] = swap(own, "seq", k)
    blocks[1] = swap(own, "seq", 1)
    for k in range(n - 2, 0, -2):
        blocks[k + 1] = swap(blocks[k], "seq", 1)
    attention, query_grad, pieces = attend(
        lengths,
        queries[0],
        out_grad[0],
        query_gain[None],
        key_gain[None],
        [blocks[k] for k in range(n)],
    )
    arrived = [pieces[0], swap(pieces[1], "seq", 1)]
    for k in range(n - 2, 0, -2):
        across = swap(pieces[k + 1], "seq", 1)
        both = (pieces[k].astype(F32) + across.astype(F32)).astype(BF16)
        arrived.append(swap(both, "seq", k))
    key_grad, value_grad, forget_grad, gains = finish(
        key_vectors[0], forget_logit[0], key_gain[None], arrived, heads
    )
    step = 1
    while step < lax.axis_size("rep"):
        gains = gains + swap(gains, "rep", step)
        step *= 2
    return (
        attention[None],
        query_grad[None],
        key_grad[None],
        value_grad[None],
        forget_grad[None],
        gains,
    )


def solution(mesh):
    return jax.shard_map(
        on_device,
        mesh=mesh,
        in_specs=(
            P("rep", "seq", None),
            P("rep", "seq", None),
            P("rep", "seq", None),
            P("rep", None, "seq"),
            P("rep", "seq", None),
            P(),
            P(),
            P("rep", None),
        ),
        out_specs=(
            P("rep", "seq", None),
            P("rep", "seq", None),
            P("rep", "seq", None),
            P("rep", "seq", None),
            P("rep", None, "seq"),
            P(),
        ),
        check_vma=False,
    )
```

```python
import functools

import jax
import jax.numpy as jnp
from jax import lax
from jax.experimental import pallas as pl
from jax.experimental.pallas import tpu as pltpu
from jax.sharding import PartitionSpec as P


TILE = 64
EPS = 1e-06
TAIL = 32
ONES = 16
CHUNK = 512
BIG = 1e30
F32 = jnp.float32
BF16 = jnp.bfloat16
VMEM = pl.BlockSpec(memory_space=pltpu.VMEM)
HBM = pl.BlockSpec(memory_space=pltpu.HBM)


def swap(value, axis, bit):
    count = lax.axis_size(axis)
    return lax.ppermute(value, axis, [(i, i ^ bit) for i in range(count)])


def struct(*shape, dtype=BF16):
    return jax.ShapeDtypeStruct(shape, dtype)


def kernel_call(kernel, operands, outs, scratch=(), limit=8 << 20, flops=1 << 20, far=0):
    in_specs = [HBM] * far + [VMEM] * (len(operands) - far)
    operands = [
        pltpu.with_memory_space_constraint(x, pltpu.HBM) if i < far else x
        for i, x in enumerate(operands)
    ]
    return pl.pallas_call(
        kernel,
        out_shape=outs,
        in_specs=in_specs,
        out_specs=jax.tree.map(lambda _: VMEM, outs),
        scratch_shapes=list(scratch),
        compiler_params=pltpu.CompilerParams(vmem_limit_bytes=limit),
        cost_estimate=pl.CostEstimate(flops=flops, bytes_accessed=1 << 20, transcendentals=0),
    )(*operands)


def dot_nn(a, b):
    return lax.dot_general(a, b, (((1,), (0,)), ((), ())), preferred_element_type=F32)


def dot_nt(a, b):
    return lax.dot_general(a, b, (((1,), (1,)), ((), ())), preferred_element_type=F32)


def iota(shape, axis):
    return lax.broadcasted_iota(jnp.int32, shape, axis)


def split3(x):
    hi = x.astype(BF16).astype(F32)
    rest = x - hi
    mid = rest.astype(BF16).astype(F32)
    return hi, mid, rest - mid


def rms(x):
    return lax.rsqrt(jnp.mean(x * x, axis=-1, keepdims=True) + EPS)


def flip(block):
    return block.astype(F32).T.astype(BF16)


def ones_where(count, test):
    shape = (count, count)
    return jnp.where(test(iota(shape, 0), iota(shape, 1)), 1.0, 0.0).astype(BF16)


def ones_rows(count):
    return jnp.where(iota((ONES, count), 0) == 0, 1.0, 0.0).astype(BF16)


def cols(h, rows):
    return slice(h * rows, (h + 1) * rows)


def chunks(wide):
    step = min(wide, CHUNK)
    return [slice(at, at + step) for at in range(0, wide, step)]


def lay_out(per_head):
    return jnp.concatenate([per_head[h : h + 1] for h in range(per_head.shape[0])], axis=1)


def log_sigmoid(x):
    small = jnp.exp(-jnp.abs(x))
    series = small * (1.0 - small * (0.5 - small * (1.0 / 3.0 - small * 0.25)))
    return jnp.minimum(x, 0.0) - jnp.where(small < 0.01, series, jnp.log(1.0 + small))


def bounds(len_ref, rows):
    me = lax.axis_index("seq")
    tiles = rows // TILE
    spans = []
    start = jnp.int32(0)
    begin = jnp.int32(0)
    for d in range(len_ref.shape[1]):
        end = start + len_ref[0, d]
        spans.append((start, end))
        begin = jnp.where(start <= me * tiles, start, begin)
        start = end
    return me, begin // tiles, spans


def first_block(low_ref):
    return lax.axis_index("seq"), low_ref[0, 0]


def is_active(me, low, k):
    b = me ^ k
    return (b <= me) & (b >= low)


def fetch(sources, targets, sem):
    copies = [pltpu.make_async_copy(*pair, sem.at[i]) for i, pair in enumerate(zip(sources, targets))]
    for copy in copies:
        copy.start()
    for copy in copies:
        copy.wait()


def near(operands):
    spaces = [pltpu.SMEM if x.dtype == jnp.int32 else pltpu.VMEM for x in operands]
    return [space(x.shape, x.dtype) for space, x in zip(spaces, operands)] + [
        pltpu.SemaphoreType.DMA((len(operands),))
    ]


def pack_kernel(*refs):
    own_ref, tail_ref, low_ref = refs[5:8]
    fetch(refs[:5], refs[8:13], refs[13])
    len_ref, k_ref, v_ref, logit_ref, gain_ref = refs[8:13]
    rows, dim = k_ref.shape
    heads = logit_ref.shape[0]
    me, low, spans = bounds(len_ref, rows)
    low_ref[...] = jnp.full(low_ref.shape, low, jnp.int32)
    key = k_ref[...].astype(F32)
    own_ref[:rows, :dim] = (key * rms(key) * gain_ref[...]).astype(BF16)
    own_ref[:rows, dim:] = v_ref[...]
    log_gate = log_sigmoid(logit_ref[...].astype(F32))
    zero = jnp.zeros((heads, rows), F32)
    parts = jnp.concatenate(list(split3(log_gate)) + [zero], axis=0).astype(BF16)

    def sums(test):
        result = dot_nn(parts, ones_where(rows, test))
        return result[:heads] + result[heads : 2 * heads] + result[2 * heads : 3 * heads]

    ahead = sums(lambda u, t: u > t)
    past = sums(lambda u, t: u <= t)
    whole = jnp.broadcast_to(past[:, rows - 1 :], (heads, rows))
    room = TAIL - 6 * heads
    row = iota((room, rows), 0)
    tile = iota((room, rows), 1) // TILE + me * (rows // TILE)
    middle = jnp.where(row < 3, 1.0, 0.0)
    for d, (start, end) in enumerate(spans):
        inside = jnp.where((tile >= start) & (tile < end), 1.0, 0.0)
        middle = jnp.where(row == 3 + d, inside, middle)
    rest = [middle] + list(split3(whole))
    tail = jnp.concatenate(list(split3(ahead)) + rest, axis=0)
    own_ref[rows:, :] = tail.astype(BF16)
    tail_ref[...] = jnp.concatenate(list(split3(-past)) + rest, axis=0).astype(BF16)


def key_columns(kaug, raw, tail):
    rows = kaug.shape[0]
    dim = raw.shape[1] // 2
    kaug[:, :dim] = raw[:rows, :dim]
    filled = jnp.concatenate([tail.astype(F32), jnp.zeros((dim - TAIL, rows), F32)], axis=0)
    kaug[:, dim:] = filled.T.astype(BF16)


def forward_block(kaug, qt, raw, tail, kt, store, mixed, causal):
    rows = kaug.shape[0]
    dim = raw.shape[1] // 2
    key_columns(kaug, raw, tail)
    both = flip(raw[:rows, :])
    kt[:dim, :] = both[:dim]
    kt[dim:, :] = ones_rows(rows)
    value_t = jnp.concatenate([both[dim:], ones_rows(rows)], axis=0)
    for part in chunks(qt.shape[1]):
        scores = dot_nn(kaug[...], qt[:, part])
        if causal:
            place = iota(scores.shape, 1)
            scores = jnp.where(iota(scores.shape, 0) <= place - place // rows * rows, scores, -BIG)
        store[:, part] = jnp.exp(scores).astype(BF16)
    for part in chunks(qt.shape[1]):
        mixed(part, dot_nn(value_t, store[:, part]))


def own_kernel(*refs):
    own_ref, tail_ref, qt, gt, acc, w_ref, kt, kaug = refs[3:11]
    fetch(refs[:3], refs[11:14], refs[14])
    q_ref, g_ref, gain_ref = refs[11:14]
    rows = q_ref.shape[0]
    dim = gain_ref.shape[1]
    heads = q_ref.shape[1] // dim
    scale = dim ** (-0.5)
    tail = tail_ref[...].astype(F32)
    past = -(tail[:heads] + tail[heads : 2 * heads] + tail[2 * heads : 3 * heads])
    parts = split3(past)
    row = iota((TAIL, rows), 0)
    doc_first = 3 * heads + 3
    docs = (row >= doc_first) & (row < TAIL - 3 * heads)
    fixed = jnp.where(docs, (tail - 1.0) * BIG, 0.0)
    for h in range(heads):
        x = q_ref[:, cols(h, dim)].astype(F32)
        normed = x * rms(x) * (gain_ref[...] * scale)
        qt[:dim, cols(h, rows)] = flip(normed.astype(BF16))
        gt[:, cols(h, rows)] = flip(g_ref[:, cols(h, dim)])
        extra = jnp.where(row < 3 * heads, jnp.where(row - row // heads * heads == h, 1.0, 0.0), fixed)
        for s in range(3):
            extra = jnp.where(row == 3 * heads + s, parts[s][h : h + 1], extra)
        qt[dim : dim + TAIL, cols(h, rows)] = extra.astype(BF16)
        qt[dim + TAIL :, cols(h, rows)] = jnp.zeros((dim - TAIL, rows), BF16)

    def mixed(part, value):
        acc[:, part] = value

    forward_block(kaug, qt, own_ref, tail_ref[...], kt, w_ref, mixed, True)


def early_kernel(n, low_ref, qt, *refs):
    half = n // 2
    raw_refs = refs[:half]
    w_ref, o_ref, kt_ref, kaug = refs[half:]
    rows = kaug.shape[0]
    me, low = first_block(low_ref)
    for s in range(half):
        raw = raw_refs[s]

        def mixed(part, value):
            o_ref[s, :, part] = value

        @pl.when(is_active(me, low, 2 * s if s else 1))
        def _():
            forward_block(
                kaug, qt, raw, raw[rows:, :], kt_ref.at[s], w_ref.at[s], mixed, False
            )


def backward_block(rows, raw, weights, factor, inner, kt, qt, gt, ds, plow, acc, kg, piece, gcol):
    dim = raw.shape[1] // 2
    for part in chunks(qt.shape[1]):
        grad = dot_nn(raw[:rows, dim:], gt[:, part])
        prob = weights[:, part].astype(F32) * factor[:, part]
        plow[:, part] = prob.astype(BF16)
        ds[:, part] = (prob * (grad - inner[:, part])).astype(BF16)
    for part in chunks(qt.shape[1]):
        acc[:, part] += dot_nn(kt[...], ds[:, part])
    key_part = dot_nt(qt[: dim + ONES, :], ds[...])
    piece[:dim, :] = key_part[:dim].astype(BF16)
    gcol[...] = -key_part[dim : dim + 8]
    kg[...] += key_part[:dim] * kt[:dim, :].astype(F32)
    piece[dim:, :] = dot_nt(gt[...], plow[...]).astype(BF16)


def idle_block(piece, gcol):
    piece[...] = jnp.zeros(piece.shape, BF16)
    gcol[...] = jnp.zeros(gcol.shape, F32)


def middle_kernel(n, heads, low_ref, qt, gt, acc0, w1_ref, o1, kt1, *refs):
    half = n // 2
    raw_refs = refs[:n]
    out_ref, acc, between_ref, log_ref, inner_ref, gcol, kg = refs[n : n + 7]
    piece_refs = refs[n + 7 : n + 7 + half]
    w, kts, kaug, ds, plow = refs[n + 7 + half :]
    rows = qt.shape[1] // heads
    dim = gt.shape[0]
    me, low = first_block(low_ref)

    wholes = []
    for k in range(n):
        tail = raw_refs[k][rows:, :].astype(F32)[TAIL - 3 * heads :]
        wholes.append(tail[:heads] + tail[heads : 2 * heads] + tail[2 * heads :])
    for k in range(n):
        total = jnp.zeros((heads, rows), F32)
        for other in range(1, n):
            if other != k:
                b = me ^ other
                total = total + jnp.where((b > (me ^ k)) & (b < me), wholes[other], 0.0)
        between_ref[k] = lay_out(total)

    acc[...] = acc0[...]
    for s in range(1, half):
        k = 2 * s + 1

        @pl.when(is_active(me, low, k))
        def _():
            root = jnp.exp(0.5 * between_ref[k])

            def mixed(part, value):
                acc[:, part] += value * root[:, part] * root[:, part]

            raw = raw_refs[k]
            forward_block(kaug, qt, raw, raw[rows:, :], kts.at[s], w.at[s], mixed, False)

    for s in range(half):
        k = 2 * s if s else 1

        @pl.when(is_active(me, low, k))
        def _():
            root = jnp.exp(0.5 * between_ref[k])
            for part in chunks(root.shape[1]):
                acc[:, part] += o1[s, :, part] * root[:, part] * root[:, part]

    eye = ones_where(rows, lambda i, j: i == j)
    for h in range(heads):
        part = cols(h, rows)
        total = acc[dim : dim + 1, part]
        mixed_t = (acc[:dim, part] * (1.0 / total)).astype(BF16)
        out_ref[:, cols(h, dim)] = dot_nt(eye, mixed_t).astype(BF16)
        log_ref[:, part] = jnp.log(total)
        product = gt[:, part].astype(F32) * mixed_t.astype(F32)
        inner_ref[:, part] = jnp.sum(product, axis=0, keepdims=True)
    acc[...] = jnp.zeros(acc.shape, F32)
    kg[...] = jnp.zeros(kg.shape, F32)
    for s in range(half - 1, -1, -1):
        k = 2 * s + 1

        @pl.when(is_active(me, low, k))
        def _():
            factor = jnp.exp(between_ref[k] - log_ref[...])
            weights, kt = (w.at[s], kts.at[s]) if s else (w1_ref.at[0], kt1.at[0])
            backward_block(
                rows, raw_refs[k], weights, factor, inner_ref, kt, qt, gt, ds, plow,
                acc, kg, piece_refs[s], gcol.at[s],
            )

        @pl.when(~is_active(me, low, k))
        def _():
            idle_block(piece_refs[s], gcol.at[s])


def late_block(s, me, low, rows, raw, source, between_ref, log_ref, inner_ref, kt, state, outs):
    qt, gt, ds, plow, acc, kg = state
    piece, gcol = outs

    @pl.when(is_active(me, low, 2 * s))
    def _():
        factor = jnp.exp(between_ref[2 * s] - log_ref[...])
        backward_block(
            rows, raw, source, factor, inner_ref, kt, qt, gt, ds, plow, acc, kg, piece, gcol
        )

    if s:

        @pl.when(~is_active(me, low, 2 * s))
        def _():
            idle_block(piece, gcol)


def late_a_kernel(rows, slots, low_ref, qt, gt, acc0, between, log_ref, inner, kg0, w1, kt1, *refs):
    count = len(slots)
    raw_refs = refs[:count]
    acc, kg, gcol = refs[count : count + 3]
    piece_refs = refs[count + 3 : 2 * count + 3]
    ds, plow = refs[2 * count + 3 :]
    me, low = first_block(low_ref)
    acc[...] = acc0[...]
    kg[...] = kg0[...]
    for i, s in enumerate(slots):
        late_block(
            s, me, low, rows, raw_refs[i], w1.at[s], between, log_ref, inner, kt1.at[s],
            (qt, gt, ds, plow, acc, kg), (piece_refs[i], gcol.at[i]),
        )


def late_b_kernel(n, slots, top, low_ref, q_ref, qgain_ref, kgain_ref, *refs):
    half = n // 2
    count = len(slots)
    qt, gt, acc0, between, log_ref, inner, kg0, w0, kt0, w1, kt1, g_odd, g_top = refs[:13]
    raw_refs = refs[13 : 13 + count]
    qgrad_ref = refs[13 + count]
    keep_ref, give_ref = refs[14 + count : 16 + count]
    piece_refs = refs[16 + count : 16 + 2 * count]
    acc, kg, ds, plow, gall = refs[16 + 2 * count :]
    rows, full = q_ref.shape
    dim = qgain_ref.shape[1]
    heads = full // dim
    scale = dim ** (-0.5)
    me, low = first_block(low_ref)
    acc[...] = acc0[...]
    kg[...] = kg0[...]
    for s in range(half):
        gall[2 * s + 1] = g_odd[s]
    for i, s in enumerate(top):
        gall[2 * s] = g_top[i]
    for i, s in enumerate(slots):
        weights, kt = (w1.at[s], kt1.at[s]) if s else (w0, kt0)
        late_block(
            s, me, low, rows, raw_refs[i], weights, between, log_ref, inner, kt,
            (qt, gt, ds, plow, acc, kg), (piece_refs[i], gall.at[2 * s]),
        )

    query_gain = jnp.zeros((1, dim), F32)
    row_sums = []
    for h in range(heads):
        x = q_ref[:, cols(h, dim)].astype(F32)
        rstd = rms(x)
        hat = x * rstd
        back = acc[:dim, cols(h, rows)].T.astype(BF16).astype(F32)
        row_sums.append(acc[dim : dim + 1, cols(h, rows)])
        query_gain = query_gain + jnp.sum(back * hat, axis=0, keepdims=True)
        back = back * (qgain_ref[...] * scale)
        mean = jnp.mean(back * hat, axis=-1, keepdims=True)
        qgrad_ref[:, cols(h, dim)] = (rstd * (back - hat * mean)).astype(BF16)
    gall[0] += jnp.concatenate(row_sums + row_sums, axis=0)[:8]
    key_gain = jnp.sum(kg[...].T, axis=0, keepdims=True) / kgain_ref[...]
    gain_row = jnp.concatenate([query_gain * scale, key_gain], axis=1)
    is_gain = iota((8, rows), 0) == heads
    later = ones_where(rows, lambda u, t: u >= t)
    stacked = jnp.concatenate([gall[k] for k in range(n)], axis=0)
    suffix = sum(dot_nn(part.astype(BF16), later) for part in split3(stacked))
    locals_ = [suffix[8 * k : 8 * k + 8] for k in range(n)]
    wholes = [jnp.broadcast_to(local[:, :1], (8, rows)) for local in locals_]
    results = []
    for k in range(n):
        total = locals_[k]
        for other in range(n):
            if other != k:
                total = total + jnp.where((me ^ other) > (me ^ k), wholes[other], 0.0)
        total = jnp.where(is_active(me, low, k), total, 0.0)
        results.append(jnp.where(is_gain, gain_row, total))
    for s in range(half):
        keep_ref[8 * s : 8 * s + 8, :] = results[2 * s]
        give_ref[8 * s : 8 * s + 8, :] = results[2 * s + 1]


def add_kernel(a_ref, b_ref, o_ref):
    o_ref[...] = (a_ref[...].astype(F32) + b_ref[...].astype(F32)).astype(BF16)


def settle_kernel(heads, keep_ref, got_ref, total_ref, gain_ref):
    total_ref[...] = keep_ref[...] + got_ref[...]
    gain_ref[...] = total_ref[heads : heads + 1, :]


def pair_kernel(a_ref, b_ref, o_ref):
    o_ref[...] = a_ref[...] + b_ref[...]


def spread_kernel(heads, total_ref, a_ref, b_ref, *outs):
    gain = a_ref[...] + b_ref[...]
    for s, out in enumerate(outs):
        rows = total_ref[8 * s : 8 * s + 8, :]
        out[...] = jnp.where(iota(rows.shape, 0) == heads, gain, rows)


def finish_kernel(half, k_ref, logit_ref, gain_ref, *refs):
    piece_refs = refs[half:-4]
    kgrad_ref, vgrad_ref, fgrad_ref, gains_ref = refs[-4:]
    dim = k_ref.shape[1]
    heads = logit_ref.shape[0]
    small = refs[0][...]
    for ref in refs[1:half]:
        small = small + ref[...]
    row = small[heads : heads + 1]
    gains_ref[...] = jnp.concatenate([row[:, :dim], row[:, dim:]], axis=0)
    total = piece_refs[0][...].astype(F32)
    for ref in piece_refs[1:]:
        total = total + ref[...].astype(F32)
    vgrad_ref[...] = total[dim:].T.astype(BF16)
    x = k_ref[...].astype(F32)
    rstd = rms(x)
    hat = x * rstd
    back = total[:dim].T * gain_ref[...]
    mean = jnp.mean(back * hat, axis=-1, keepdims=True)
    kgrad_ref[...] = (rstd * (back - hat * mean)).astype(BF16)
    logit = logit_ref[...].astype(F32)
    fgrad_ref[...] = small[:heads] * (1.0 / (1.0 + jnp.exp(logit)))


def whole_step(queries, key_vectors, values, forget_logit, out_grad, query_gain, key_gain, lengths):
    n = lax.axis_size("seq")
    half = n // 2
    rows, full = queries.shape[1:]
    dim = query_gain.shape[0]
    heads = full // dim
    wide = heads * rows
    width = 2 * dim
    tall = dim + ONES
    query, grad, key, logit = queries[0], out_grad[0], key_vectors[0], forget_logit[0]
    qgain, kgain = query_gain[None], key_gain[None]
    matmul = 2 * rows * wide * width
    head_row = struct(heads, rows, dtype=F32)
    line = struct(1, wide, dtype=F32)
    state = struct(tall, wide, dtype=F32)
    key_sum = struct(dim, rows, dtype=F32)
    piece = struct(rows, width)
    wide_scratch = pltpu.VMEM((rows, wide), BF16)

    inputs = [lengths, key, values[0], logit, kgain]
    own, own_tail, low = kernel_call(
        pack_kernel, inputs, (
            struct(rows + TAIL, width), struct(TAIL, rows), struct(8, 128, dtype=jnp.int32),
        ),
        near(inputs), far=5,
    )
    blocks = {0: own}
    for k in range(n - 2, 0, -2):
        blocks[k] = swap(own, "seq", k)
    blocks[1] = swap(own, "seq", 1)
    for k in range(n - 2, 0, -2):
        blocks[k + 1] = swap(blocks[k], "seq", 1)

    qt, gt, acc, w0, kt0 = kernel_call(
        own_kernel, [query, grad, qgain, own, own_tail],
        (struct(width, wide), struct(dim, wide), state, struct(rows, wide), struct(tall, rows)),
        [pltpu.VMEM((rows, width), BF16)] + near([query, grad, qgain]),
        flops=2 * matmul,
        far=3,
    )
    early = [1] + [2 * s for s in range(1, half)]
    w1, o1, kt1 = kernel_call(
        functools.partial(early_kernel, n),
        [low, qt] + [blocks[k] for k in early],
        (
            struct(half, rows, wide),
            struct(half, tall, wide, dtype=F32),
            struct(half, tall, rows),
        ),
        [pltpu.VMEM((rows, width), BF16)],
        flops=2 * half * matmul,
    )
    results = kernel_call(
        functools.partial(middle_kernel, n, heads),
        [low, qt, gt, acc, w1, o1, kt1] + [blocks[k] for k in range(n)],
        (
            struct(rows, full), state, struct(n, 1, wide, dtype=F32), line, line,
            struct(half, 8, rows, dtype=F32), key_sum,
        )
        + (piece,) * half,
        [
            pltpu.VMEM((half, rows, wide), BF16),
            pltpu.VMEM((half, tall, rows), BF16),
            pltpu.VMEM((rows, width), BF16),
            wide_scratch,
            wide_scratch,
        ],
        limit=(8 << 20) + n * (1 << 19),
        flops=6 * half * matmul,
    )
    attention, acc, between, log_total, inner, gate_odd, key_acc = results[:7]
    odd = results[7:]
    across = [swap(odd[s], "seq", 1) for s in range(half)]

    top = list(range(half - 1, half // 2 - 1, -1))
    bottom = list(range(half // 2 - 1, -1, -1))
    results = kernel_call(
        functools.partial(late_a_kernel, rows, top),
        [low, qt, gt, acc, between, log_total, inner, key_acc, w1, kt1]
        + [blocks[2 * s] for s in top],
        (state, key_sum, struct(len(top), 8, rows, dtype=F32)) + (piece,) * len(top),
        [wide_scratch, wide_scratch],
        flops=4 * len(top) * matmul,
    )
    acc, key_acc, gate_top = results[:3]
    even = dict(zip(top, results[3:]))
    results = kernel_call(
        functools.partial(late_b_kernel, n, bottom, top),
        [low, query, qgain, kgain, qt, gt, acc, between, log_total, inner, key_acc]
        + [w0, kt0, w1, kt1, gate_odd, gate_top]
        + [blocks[2 * s] for s in bottom],
        (struct(rows, full),)
        + (struct(8 * half, rows, dtype=F32),) * 2
        + (piece,) * len(bottom),
        [
            pltpu.VMEM((tall, wide), F32),
            pltpu.VMEM((dim, rows), F32),
            wide_scratch,
            wide_scratch,
            pltpu.VMEM((n, 8, rows), F32),
        ],
        flops=4 * len(bottom) * matmul,
    )
    query_grad, keep, give = results[:3]
    even.update(zip(bottom, results[3:]))

    arrived = [even[0], across[0]]
    for s in range(half - 1, 0, -1):
        both = kernel_call(add_kernel, [even[s], across[s]], piece)
        arrived.append(swap(both, "seq", 2 * s))

    gain_line = struct(1, width, dtype=F32)
    eight = struct(8, rows, dtype=F32)
    total, gain = kernel_call(
        functools.partial(settle_kernel, heads), [keep, swap(give, "seq", 1)],
        (struct(8 * half, rows, dtype=F32), gain_line),
    )
    bit = 1
    while 2 * bit < lax.axis_size("rep"):
        gain = kernel_call(pair_kernel, [gain, swap(gain, "rep", bit)], gain_line)
        bit *= 2
    smalls = kernel_call(
        functools.partial(spread_kernel, heads),
        [total, gain, swap(gain, "rep", bit)], (eight,) * half,
    )
    smalls = [smalls[0]] + [swap(smalls[s], "seq", 2 * s) for s in range(1, half)]
    key_grad, value_grad, forget_grad, gains = kernel_call(
        functools.partial(finish_kernel, half), [key, logit, kgain] + smalls + arrived,
        (struct(rows, dim), struct(rows, dim), head_row, struct(2, dim, dtype=F32)),
    )
    return (
        attention[None],
        query_grad[None],
        key_grad[None],
        value_grad[None],
        forget_grad[None],
        gains,
    )


def solution(mesh):
    return jax.shard_map(
        whole_step,
        mesh=mesh,
        in_specs=(
            P("rep", "seq", None),
            P("rep", "seq", None),
            P("rep", "seq", None),
            P("rep", None, "seq"),
            P("rep", "seq", None),
            P(),
            P(),
            P("rep", None),
        ),
        out_specs=(
            P("rep", "seq", None),
            P("rep", "seq", None),
            P("rep", "seq", None),
            P("rep", "seq", None),
            P("rep", None, "seq"),
            P(),
        ),
        check_vma=False,
    )
```

```python
import functools

import jax
import jax.numpy as jnp
from jax import lax
from jax.experimental import pallas as pl
from jax.experimental.pallas import tpu as pltpu
from jax.sharding import PartitionSpec as P


TILE = 64
EPS = 1e-06
TAIL = 32
ONES = 16
CHUNK = 512
BIG = 1e30
F32 = jnp.float32
BF16 = jnp.bfloat16
VMEM = pl.BlockSpec(memory_space=pltpu.VMEM)
HBM = pl.BlockSpec(memory_space=pltpu.HBM)


def swap(value, axis, bit):
    count = lax.axis_size(axis)
    return lax.ppermute(value, axis, [(i, i ^ bit) for i in range(count)])


def swap_both(value, bit):
    count = lax.axis_size("seq") * lax.axis_size("rep")
    return lax.ppermute(value, ("seq", "rep"), [(i, i ^ bit) for i in range(count)])


def struct(*shape, dtype=BF16):
    return jax.ShapeDtypeStruct(shape, dtype)


def kernel_call(kernel, operands, outs, scratch=(), limit=8 << 20, flops=1 << 20, far=0):
    in_specs = [HBM] * far + [VMEM] * (len(operands) - far)
    operands = [
        pltpu.with_memory_space_constraint(x, pltpu.HBM) if i < far else x
        for i, x in enumerate(operands)
    ]
    return pl.pallas_call(
        kernel,
        out_shape=outs,
        in_specs=in_specs,
        out_specs=jax.tree.map(lambda _: VMEM, outs),
        scratch_shapes=list(scratch),
        compiler_params=pltpu.CompilerParams(vmem_limit_bytes=limit),
        cost_estimate=pl.CostEstimate(flops=flops, bytes_accessed=1 << 20, transcendentals=0),
    )(*operands)


def dot_nn(a, b):
    return lax.dot_general(a, b, (((1,), (0,)), ((), ())), preferred_element_type=F32)


def dot_nt(a, b):
    return lax.dot_general(a, b, (((1,), (1,)), ((), ())), preferred_element_type=F32)


def iota(shape, axis):
    return lax.broadcasted_iota(jnp.int32, shape, axis)


def split3(x):
    hi = x.astype(BF16).astype(F32)
    rest = x - hi
    mid = rest.astype(BF16).astype(F32)
    return hi, mid, rest - mid


def rms(x):
    return lax.rsqrt(jnp.mean(x * x, axis=-1, keepdims=True) + EPS)


def flip(block):
    return block.astype(F32).T.astype(BF16)


def ones_where(count, test):
    shape = (count, count)
    return jnp.where(test(iota(shape, 0), iota(shape, 1)), 1.0, 0.0).astype(BF16)


def ones_rows(count):
    return jnp.where(iota((ONES, count), 0) == 0, 1.0, 0.0).astype(BF16)


def cols(h, rows):
    return slice(h * rows, (h + 1) * rows)


def chunks(wide):
    step = min(wide, CHUNK)
    return [slice(at, at + step) for at in range(0, wide, step)]


def lay_out(per_head):
    return jnp.concatenate([per_head[h : h + 1] for h in range(per_head.shape[0])], axis=1)


def log_sigmoid(x):
    small = jnp.exp(-jnp.abs(x))
    series = small * (1.0 - small * (0.5 - small * (1.0 / 3.0 - small * 0.25)))
    return jnp.minimum(x, 0.0) - jnp.where(small < 0.01, series, jnp.log(1.0 + small))


def bounds(len_ref, rows):
    me = lax.axis_index("seq")
    tiles = rows // TILE
    spans = []
    start = jnp.int32(0)
    begin = jnp.int32(0)
    for d in range(len_ref.shape[1]):
        end = start + len_ref[0, d]
        spans.append((start, end))
        begin = jnp.where(start <= me * tiles, start, begin)
        start = end
    return me, begin // tiles, spans


def first_block(low_ref):
    return lax.axis_index("seq"), low_ref[0, 0]


def is_active(me, low, k):
    b = me ^ k
    return (b <= me) & (b >= low)


def fetch(sources, targets, sem):
    copies = [pltpu.make_async_copy(*pair, sem.at[i]) for i, pair in enumerate(zip(sources, targets))]
    for copy in copies:
        copy.start()
    for copy in copies:
        copy.wait()


def near(operands):
    spaces = [pltpu.SMEM if x.dtype == jnp.int32 else pltpu.VMEM for x in operands]
    return [space(x.shape, x.dtype) for space, x in zip(spaces, operands)] + [
        pltpu.SemaphoreType.DMA((len(operands),))
    ]


def pack_kernel(*refs):
    own_ref, tail_ref, low_ref = refs[5:8]
    fetch(refs[:5], refs[8:13], refs[13])
    len_ref, k_ref, v_ref, logit_ref, gain_ref = refs[8:13]
    rows, dim = k_ref.shape
    heads = logit_ref.shape[0]
    me, low, spans = bounds(len_ref, rows)
    low_ref[...] = jnp.full(low_ref.shape, low, jnp.int32)
    key = k_ref[...].astype(F32)
    own_ref[:rows, :dim] = (key * rms(key) * gain_ref[...]).astype(BF16)
    own_ref[:rows, dim:] = v_ref[...]
    log_gate = log_sigmoid(logit_ref[...].astype(F32))
    zero = jnp.zeros((heads, rows), F32)
    parts = jnp.concatenate(list(split3(log_gate)) + [zero], axis=0).astype(BF16)

    def sums(test):
        result = dot_nn(parts, ones_where(rows, test))
        return result[:heads] + result[heads : 2 * heads] + result[2 * heads : 3 * heads]

    ahead = sums(lambda u, t: u > t)
    past = sums(lambda u, t: u <= t)
    whole = jnp.broadcast_to(past[:, rows - 1 :], (heads, rows))
    room = TAIL - 6 * heads
    row = iota((room, rows), 0)
    tile = iota((room, rows), 1) // TILE + me * (rows // TILE)
    middle = jnp.where(row < 3, 1.0, 0.0)
    for d, (start, end) in enumerate(spans):
        inside = jnp.where((tile >= start) & (tile < end), 1.0, 0.0)
        middle = jnp.where(row == 3 + d, inside, middle)
    rest = [middle] + list(split3(whole))
    tail = jnp.concatenate(list(split3(ahead)) + rest, axis=0)
    own_ref[rows:, :] = tail.astype(BF16)
    tail_ref[...] = jnp.concatenate(list(split3(-past)) + rest, axis=0).astype(BF16)


def key_columns(kaug, raw, tail):
    rows = kaug.shape[0]
    dim = raw.shape[1] // 2
    kaug[:, :dim] = raw[:rows, :dim]
    filled = jnp.concatenate([tail.astype(F32), jnp.zeros((dim - TAIL, rows), F32)], axis=0)
    kaug[:, dim:] = filled.T.astype(BF16)


def forward_block(kaug, qt, raw, tail, kt, store, mixed, causal):
    rows = kaug.shape[0]
    dim = raw.shape[1] // 2
    key_columns(kaug, raw, tail)
    both = flip(raw[:rows, :])
    kt[:dim, :] = both[:dim]
    kt[dim:, :] = ones_rows(rows)
    value_t = jnp.concatenate([both[dim:], ones_rows(rows)], axis=0)
    for part in chunks(qt.shape[1]):
        scores = dot_nn(kaug[...], qt[:, part])
        if causal:
            place = iota(scores.shape, 1)
            scores = jnp.where(iota(scores.shape, 0) <= place - place // rows * rows, scores, -BIG)
        store[:, part] = jnp.exp(scores).astype(BF16)
    for part in chunks(qt.shape[1]):
        mixed(part, dot_nn(value_t, store[:, part]))


def own_kernel(*refs):
    own_ref, tail_ref, qt, gt, acc, w_ref, kt, kaug = refs[3:11]
    fetch(refs[:3], refs[11:14], refs[14])
    q_ref, g_ref, gain_ref = refs[11:14]
    rows = q_ref.shape[0]
    dim = gain_ref.shape[1]
    heads = q_ref.shape[1] // dim
    scale = dim ** (-0.5)
    tail = tail_ref[...].astype(F32)
    past = -(tail[:heads] + tail[heads : 2 * heads] + tail[2 * heads : 3 * heads])
    parts = split3(past)
    row = iota((TAIL, rows), 0)
    doc_first = 3 * heads + 3
    docs = (row >= doc_first) & (row < TAIL - 3 * heads)
    fixed = jnp.where(docs, (tail - 1.0) * BIG, 0.0)
    for h in range(heads):
        x = q_ref[:, cols(h, dim)].astype(F32)
        normed = x * rms(x) * (gain_ref[...] * scale)
        qt[:dim, cols(h, rows)] = flip(normed.astype(BF16))
        gt[:, cols(h, rows)] = flip(g_ref[:, cols(h, dim)])
        extra = jnp.where(row < 3 * heads, jnp.where(row - row // heads * heads == h, 1.0, 0.0), fixed)
        for s in range(3):
            extra = jnp.where(row == 3 * heads + s, parts[s][h : h + 1], extra)
        qt[dim : dim + TAIL, cols(h, rows)] = extra.astype(BF16)
        qt[dim + TAIL :, cols(h, rows)] = jnp.zeros((dim - TAIL, rows), BF16)

    def mixed(part, value):
        acc[:, part] = value

    forward_block(kaug, qt, own_ref, tail_ref[...], kt, w_ref, mixed, True)


def early_kernel(n, low_ref, qt, *refs):
    half = n // 2
    raw_refs = refs[:half]
    w_ref, o_ref, kt_ref, kaug = refs[half:]
    rows = kaug.shape[0]
    me, low = first_block(low_ref)
    for s in range(half):
        raw = raw_refs[s]

        def mixed(part, value):
            o_ref[s, :, part] = value

        @pl.when(is_active(me, low, 2 * s if s else 1))
        def _():
            forward_block(
                kaug, qt, raw, raw[rows:, :], kt_ref.at[s], w_ref.at[s], mixed, False
            )


def backward_block(rows, raw, weights, factor, inner, kt, qt, gt, ds, plow, acc, kg, piece, gcol):
    dim = raw.shape[1] // 2
    for part in chunks(qt.shape[1]):
        grad = dot_nn(raw[:rows, dim:], gt[:, part])
        prob = weights[:, part].astype(F32) * factor[:, part]
        plow[:, part] = prob.astype(BF16)
        ds[:, part] = (prob * (grad - inner[:, part])).astype(BF16)
    for part in chunks(qt.shape[1]):
        acc[:, part] += dot_nn(kt[...], ds[:, part])
    key_part = dot_nt(qt[: dim + ONES, :], ds[...])
    piece[:dim, :] = key_part[:dim].astype(BF16)
    gcol[...] = -key_part[dim : dim + 8]
    kg[...] += key_part[:dim] * kt[:dim, :].astype(F32)
    piece[dim:, :] = dot_nt(gt[...], plow[...]).astype(BF16)


def idle_block(piece, gcol):
    piece[...] = jnp.zeros(piece.shape, BF16)
    gcol[...] = jnp.zeros(gcol.shape, F32)


def middle_kernel(n, heads, low_ref, qt, gt, acc0, w1_ref, o1, kt1, *refs):
    half = n // 2
    raw_refs = refs[:n]
    out_ref, acc, between_ref, log_ref, inner_ref, gcol, kg = refs[n : n + 7]
    piece_refs = refs[n + 7 : n + 7 + half]
    w, kts, kaug, ds, plow = refs[n + 7 + half :]
    rows = qt.shape[1] // heads
    dim = gt.shape[0]
    me, low = first_block(low_ref)

    wholes = []
    for k in range(n):
        tail = raw_refs[k][rows:, :].astype(F32)[TAIL - 3 * heads :]
        wholes.append(tail[:heads] + tail[heads : 2 * heads] + tail[2 * heads :])
    for k in range(n):
        total = jnp.zeros((heads, rows), F32)
        for other in range(1, n):
            if other != k:
                b = me ^ other
                total = total + jnp.where((b > (me ^ k)) & (b < me), wholes[other], 0.0)
        between_ref[k] = lay_out(total)

    acc[...] = acc0[...]
    for s in range(1, half):
        k = 2 * s + 1

        @pl.when(is_active(me, low, k))
        def _():
            root = jnp.exp(0.5 * between_ref[k])

            def mixed(part, value):
                acc[:, part] += value * root[:, part] * root[:, part]

            raw = raw_refs[k]
            forward_block(kaug, qt, raw, raw[rows:, :], kts.at[s], w.at[s], mixed, False)

    for s in range(half):
        k = 2 * s if s else 1

        @pl.when(is_active(me, low, k))
        def _():
            root = jnp.exp(0.5 * between_ref[k])
            for part in chunks(root.shape[1]):
                acc[:, part] += o1[s, :, part] * root[:, part] * root[:, part]

    eye = ones_where(rows, lambda i, j: i == j)
    for h in range(heads):
        part = cols(h, rows)
        total = acc[dim : dim + 1, part]
        mixed_t = (acc[:dim, part] * (1.0 / total)).astype(BF16)
        out_ref[:, cols(h, dim)] = dot_nt(eye, mixed_t).astype(BF16)
        log_ref[:, part] = jnp.log(total)
        product = gt[:, part].astype(F32) * mixed_t.astype(F32)
        inner_ref[:, part] = jnp.sum(product, axis=0, keepdims=True)
    acc[...] = jnp.zeros(acc.shape, F32)
    kg[...] = jnp.zeros(kg.shape, F32)
    for s in range(half - 1, -1, -1):
        k = 2 * s + 1

        @pl.when(is_active(me, low, k))
        def _():
            factor = jnp.exp(between_ref[k] - log_ref[...])
            weights, kt = (w.at[s], kts.at[s]) if s else (w1_ref.at[0], kt1.at[0])
            backward_block(
                rows, raw_refs[k], weights, factor, inner_ref, kt, qt, gt, ds, plow,
                acc, kg, piece_refs[s], gcol.at[s],
            )

        @pl.when(~is_active(me, low, k))
        def _():
            idle_block(piece_refs[s], gcol.at[s])


def late_block(s, me, low, rows, raw, source, between_ref, log_ref, inner_ref, kt, state, outs):
    qt, gt, ds, plow, acc, kg = state
    piece, gcol = outs

    @pl.when(is_active(me, low, 2 * s))
    def _():
        factor = jnp.exp(between_ref[2 * s] - log_ref[...])
        backward_block(
            rows, raw, source, factor, inner_ref, kt, qt, gt, ds, plow, acc, kg, piece, gcol
        )

    if s:

        @pl.when(~is_active(me, low, 2 * s))
        def _():
            idle_block(piece, gcol)


def late_kernel(n, low_ref, kgain_ref, qgain_ref, *refs):
    half = n // 2
    qt, gt, acc0, between, log_ref, inner, kg0, w0, kt0, w1, kt1, g_odd = refs[:12]
    raw_refs = refs[12 : 12 + half]
    acc, keep_ref, give_ref, gain_ref = refs[12 + half : 16 + half]
    piece_refs = refs[16 + half : 16 + 2 * half]
    kg, ds, plow, gall = refs[16 + 2 * half :]
    rows = ds.shape[0]
    dim = qgain_ref.shape[1]
    heads = qt.shape[1] // rows
    me, low = first_block(low_ref)
    acc[...] = acc0[...]
    kg[...] = kg0[...]
    for s in range(half):
        gall[2 * s + 1] = g_odd[s]
    for s in range(half - 1, -1, -1):
        weights, kt = (w1.at[s], kt1.at[s]) if s else (w0, kt0)
        late_block(
            s, me, low, rows, raw_refs[s], weights, between, log_ref, inner, kt,
            (qt, gt, ds, plow, acc, kg), (piece_refs[s], gall.at[2 * s]),
        )

    qg = jnp.zeros((dim, rows), F32)
    row_sums = []
    for h in range(heads):
        part = cols(h, rows)
        qg = qg + acc[:dim, part] * qt[:dim, part].astype(F32)
        row_sums.append(acc[dim : dim + 1, part])
    gall[0] += jnp.concatenate(row_sums + row_sums, axis=0)[:8]
    query_gain = jnp.sum(qg.T, axis=0, keepdims=True) / qgain_ref[...]
    key_gain = jnp.sum(kg[...].T, axis=0, keepdims=True) / kgain_ref[...]
    gain_row = jnp.concatenate([query_gain, key_gain], axis=1)
    gain_ref[...] = gain_row
    is_gain = iota((8, rows), 0) == heads
    later = ones_where(rows, lambda u, t: u >= t)
    stacked = jnp.concatenate([gall[k] for k in range(n)], axis=0)
    suffix = sum(dot_nn(part.astype(BF16), later) for part in split3(stacked))
    locals_ = [suffix[8 * k : 8 * k + 8] for k in range(n)]
    wholes = [jnp.broadcast_to(local[:, :1], (8, rows)) for local in locals_]
    results = []
    for k in range(n):
        total = locals_[k]
        for other in range(n):
            if other != k:
                total = total + jnp.where((me ^ other) > (me ^ k), wholes[other], 0.0)
        total = jnp.where(is_active(me, low, k), total, 0.0)
        results.append(jnp.where(is_gain, gain_row, total))
    for s in range(half):
        keep_ref[8 * s : 8 * s + 8, :] = results[2 * s]
        give_ref[8 * s : 8 * s + 8, :] = results[2 * s + 1]


def query_kernel(q_ref, qgain_ref, acc, qgrad_ref):
    rows = q_ref.shape[0]
    dim = qgain_ref.shape[1]
    scale = dim ** (-0.5)
    for h in range(q_ref.shape[1] // dim):
        x = q_ref[:, cols(h, dim)].astype(F32)
        rstd = rms(x)
        hat = x * rstd
        back = acc[:dim, cols(h, rows)].T.astype(BF16).astype(F32) * (qgain_ref[...] * scale)
        mean = jnp.mean(back * hat, axis=-1, keepdims=True)
        qgrad_ref[:, cols(h, dim)] = (rstd * (back - hat * mean)).astype(BF16)


def add_kernel(a_ref, b_ref, o_ref):
    o_ref[...] = (a_ref[...].astype(F32) + b_ref[...].astype(F32)).astype(BF16)


def settle_kernel(heads, keep_ref, got_ref, a_ref, b_ref, total_ref, gain_ref):
    total_ref[...] = keep_ref[...] + got_ref[...]
    gain_ref[...] = total_ref[heads : heads + 1, :] + a_ref[...] + b_ref[...]


def pair_kernel(a_ref, b_ref, o_ref):
    o_ref[...] = a_ref[...] + b_ref[...]


def spread_kernel(heads, total_ref, gain_ref, *outs):
    for s, out in enumerate(outs):
        rows = total_ref[8 * s : 8 * s + 8, :]
        out[...] = jnp.where(iota(rows.shape, 0) == heads, gain_ref[...], rows)


def finish_kernel(k_ref, gain_ref, *refs):
    piece_refs = refs[:-2]
    kgrad_ref, vgrad_ref = refs[-2:]
    dim = k_ref.shape[1]
    total = piece_refs[0][...].astype(F32)
    for ref in piece_refs[1:]:
        total = total + ref[...].astype(F32)
    vgrad_ref[...] = total[dim:].T.astype(BF16)
    x = k_ref[...].astype(F32)
    rstd = rms(x)
    hat = x * rstd
    back = total[:dim].T * gain_ref[...]
    mean = jnp.mean(back * hat, axis=-1, keepdims=True)
    kgrad_ref[...] = (rstd * (back - hat * mean)).astype(BF16)


def forget_kernel(logit_ref, *refs):
    small_refs = refs[:-2]
    fgrad_ref, gains_ref = refs[-2:]
    heads = logit_ref.shape[0]
    small = small_refs[0][...]
    for ref in small_refs[1:]:
        small = small + ref[...]
    logit = logit_ref[...].astype(F32)
    fgrad_ref[...] = small[:heads] * (1.0 / (1.0 + jnp.exp(logit)))
    row = small[heads : heads + 1]
    dim = row.shape[1] // 2
    gains_ref[...] = jnp.concatenate([row[:, :dim], row[:, dim:]], axis=0)


def whole_step(queries, key_vectors, values, forget_logit, out_grad, query_gain, key_gain, lengths):
    n = lax.axis_size("seq")
    half = n // 2
    rows, full = queries.shape[1:]
    dim = query_gain.shape[0]
    heads = full // dim
    wide = heads * rows
    width = 2 * dim
    tall = dim + ONES
    query, grad, key, logit = queries[0], out_grad[0], key_vectors[0], forget_logit[0]
    qgain, kgain = query_gain[None], key_gain[None]
    matmul = 2 * rows * wide * width
    head_row = struct(heads, rows, dtype=F32)
    line = struct(1, wide, dtype=F32)
    state = struct(tall, wide, dtype=F32)
    key_sum = struct(dim, rows, dtype=F32)
    piece = struct(rows, width)
    wide_scratch = pltpu.VMEM((rows, wide), BF16)

    inputs = [lengths, key, values[0], logit, kgain]
    own, own_tail, low = kernel_call(
        pack_kernel, inputs, (
            struct(rows + TAIL, width), struct(TAIL, rows), struct(8, 128, dtype=jnp.int32),
        ),
        near(inputs), far=5,
    )
    blocks = {0: own}
    gather_order = [2] + list(range(n - 2, 2, -2))
    for k in gather_order:
        blocks[k] = swap(own, "seq", k)
    blocks[1] = swap(own, "seq", 1)
    for k in gather_order:
        blocks[k + 1] = swap(blocks[k], "seq", 1)

    qt, gt, acc, w0, kt0 = kernel_call(
        own_kernel, [query, grad, qgain, own, own_tail],
        (struct(width, wide), struct(dim, wide), state, struct(rows, wide), struct(tall, rows)),
        [pltpu.VMEM((rows, width), BF16)] + near([query, grad, qgain]),
        flops=2 * matmul,
        far=3,
    )
    early = [1] + [2 * s for s in range(1, half)]
    w1, o1, kt1 = kernel_call(
        functools.partial(early_kernel, n),
        [low, qt] + [blocks[k] for k in early],
        (
            struct(half, rows, wide),
            struct(half, tall, wide, dtype=F32),
            struct(half, tall, rows),
        ),
        [pltpu.VMEM((rows, width), BF16)],
        flops=2 * half * matmul,
    )
    results = kernel_call(
        functools.partial(middle_kernel, n, heads),
        [low, qt, gt, acc, w1, o1, kt1] + [blocks[k] for k in range(n)],
        (
            struct(rows, full), state, struct(n, 1, wide, dtype=F32), line, line,
            struct(half, 8, rows, dtype=F32), key_sum,
        )
        + (piece,) * half,
        [
            pltpu.VMEM((half, rows, wide), BF16),
            pltpu.VMEM((half, tall, rows), BF16),
            pltpu.VMEM((rows, width), BF16),
            wide_scratch,
            wide_scratch,
        ],
        limit=(8 << 20) + n * (1 << 19),
        flops=6 * half * matmul,
    )
    attention, acc, between, log_total, inner, gate_odd, key_acc = results[:7]
    odd = results[7:]
    order = list(range(half - 1, 0, -1))
    across = {s: swap(odd[s], "seq", 1) for s in order + [0]}

    results = kernel_call(
        functools.partial(late_kernel, n),
        [low, kgain, qgain, qt, gt, acc, between, log_total, inner, key_acc]
        + [w0, kt0, w1, kt1, gate_odd]
        + [blocks[2 * s] for s in range(half)],
        (
            state, struct(8 * half, rows, dtype=F32), struct(8 * half, rows, dtype=F32),
            struct(1, width, dtype=F32),
        )
        + (piece,) * half,
        [pltpu.VMEM((dim, rows), F32), wide_scratch, wide_scratch, pltpu.VMEM((n, 8, rows), F32)],
        flops=4 * half * matmul,
    )
    acc, keep, give, gain = results[:4]
    even = results[4:]

    gain_line = struct(1, width, dtype=F32)
    eight = struct(8, rows, dtype=F32)
    got = swap(give, "seq", 1)
    near_gain = swap(gain, "rep", 1)
    far_gain = swap_both(gain, lax.axis_size("rep") + 1)
    query_grad = kernel_call(query_kernel, [query, qgain, acc], struct(rows, full), flops=matmul)
    arrived = [even[0], across[0]]
    for s in order:
        both = kernel_call(add_kernel, [even[s], across[s]], piece)
        arrived.append(swap(both, "seq", 2 * s))

    total, gain = kernel_call(
        functools.partial(settle_kernel, heads), [keep, got, near_gain, far_gain],
        (struct(8 * half, rows, dtype=F32), gain_line),
    )
    bit = 2
    while bit < lax.axis_size("rep"):
        gain = kernel_call(pair_kernel, [gain, swap(gain, "rep", bit)], gain_line)
        bit *= 2
    smalls = kernel_call(functools.partial(spread_kernel, heads), [total, gain], (eight,) * half)
    smalls = [smalls[0]] + [swap(smalls[s], "seq", 2 * s) for s in range(1, half)]
    key_grad, value_grad = kernel_call(
        finish_kernel, [key, kgain] + arrived, (struct(rows, dim), struct(rows, dim)),
        flops=matmul,
    )
    forget_grad, gains = kernel_call(
        forget_kernel, [logit] + smalls, (head_row, struct(2, dim, dtype=F32))
    )
    return (
        attention[None],
        query_grad[None],
        key_grad[None],
        value_grad[None],
        forget_grad[None],
        gains,
    )


def solution(mesh):
    return jax.shard_map(
        whole_step,
        mesh=mesh,
        in_specs=(
            P("rep", "seq", None),
            P("rep", "seq", None),
            P("rep", "seq", None),
            P("rep", None, "seq"),
            P("rep", "seq", None),
            P(),
            P(),
            P("rep", None),
        ),
        out_specs=(
            P("rep", "seq", None),
            P("rep", "seq", None),
            P("rep", "seq", None),
            P("rep", "seq", None),
            P("rep", None, "seq"),
            P(),
        ),
        check_vma=False,
    )
```

```python
import functools

import jax
import jax.numpy as jnp
from jax import lax
from jax.experimental import pallas as pl
from jax.experimental.pallas import tpu as pltpu
from jax.sharding import PartitionSpec as P


TILE = 64
EPS = 1e-06
TAIL = 16
ONES = 16
CHUNK = 512
BIG = 1e30
F32 = jnp.float32
BF16 = jnp.bfloat16
VMEM = pl.BlockSpec(memory_space=pltpu.VMEM)
HBM = pl.BlockSpec(memory_space=pltpu.HBM)


def swap(value, axis, bit):
    count = lax.axis_size(axis)
    return lax.ppermute(value, axis, [(i, i ^ bit) for i in range(count)])


def struct(*shape, dtype=BF16):
    return jax.ShapeDtypeStruct(shape, dtype)


def kernel_call(kernel, operands, outs, scratch=(), limit=8 << 20, flops=1 << 20, far=0):
    in_specs = [HBM] * far + [VMEM] * (len(operands) - far)
    operands = [
        pltpu.with_memory_space_constraint(x, pltpu.HBM) if i < far else x
        for i, x in enumerate(operands)
    ]
    return pl.pallas_call(
        kernel,
        out_shape=outs,
        in_specs=in_specs,
        out_specs=jax.tree.map(lambda _: VMEM, outs),
        scratch_shapes=list(scratch),
        compiler_params=pltpu.CompilerParams(vmem_limit_bytes=limit),
        cost_estimate=pl.CostEstimate(flops=flops, bytes_accessed=1 << 20, transcendentals=0),
    )(*operands)


def dot_nn(a, b):
    return lax.dot_general(a, b, (((1,), (0,)), ((), ())), preferred_element_type=F32)


def dot_nt(a, b):
    return lax.dot_general(a, b, (((1,), (1,)), ((), ())), preferred_element_type=F32)


def iota(shape, axis):
    return lax.broadcasted_iota(jnp.int32, shape, axis)


def split3(x):
    hi = x.astype(BF16).astype(F32)
    rest = x - hi
    mid = rest.astype(BF16).astype(F32)
    return hi, mid, rest - mid


def rms(x):
    return lax.rsqrt(jnp.mean(x * x, axis=-1, keepdims=True) + EPS)


def flip(block):
    return block.astype(F32).T.astype(BF16)


def ones_where(count, test):
    shape = (count, count)
    return jnp.where(test(iota(shape, 0), iota(shape, 1)), 1.0, 0.0).astype(BF16)


def ones_rows(count):
    return jnp.where(iota((ONES, count), 0) == 0, 1.0, 0.0).astype(BF16)


def cols(h, rows):
    return slice(h * rows, (h + 1) * rows)


def chunks(wide):
    step = min(wide, CHUNK)
    return [slice(at, at + step) for at in range(0, wide, step)]


def lay_out(per_head):
    return jnp.concatenate([per_head[h : h + 1] for h in range(per_head.shape[0])], axis=1)


def log_sigmoid(x):
    small = jnp.exp(-jnp.abs(x))
    series = small * (1.0 - small * (0.5 - small * (1.0 / 3.0 - small * 0.25)))
    return jnp.minimum(x, 0.0) - jnp.where(small < 0.01, series, jnp.log(1.0 + small))


def bounds(len_ref, rows):
    me = lax.axis_index("seq")
    tiles = rows // TILE
    spans = []
    start = jnp.int32(0)
    begin = jnp.int32(0)
    for d in range(len_ref.shape[1]):
        end = start + len_ref[0, d]
        spans.append((start, end))
        begin = jnp.where(start <= me * tiles, start, begin)
        start = end
    return me, begin // tiles, spans


def first_block(low_ref):
    return lax.axis_index("seq"), low_ref[0, 0]


def is_active(me, low, k):
    b = me ^ k
    return (b <= me) & (b >= low)


def fetch(sources, targets, sem):
    copies = [pltpu.make_async_copy(*pair, sem.at[i]) for i, pair in enumerate(zip(sources, targets))]
    for copy in copies:
        copy.start()
    for copy in copies:
        copy.wait()


def near(operands):
    spaces = [pltpu.SMEM if x.dtype == jnp.int32 else pltpu.VMEM for x in operands]
    return [space(x.shape, x.dtype) for space, x in zip(spaces, operands)] + [
        pltpu.SemaphoreType.DMA((len(operands),))
    ]


def pack_kernel(*refs):
    own_ref, share_ref, tail_ref, low_ref = refs[5:9]
    fetch(refs[:5], refs[9:14], refs[14])
    len_ref, k_ref, v_ref, logit_ref, gain_ref = refs[9:14]
    rows, dim = k_ref.shape
    heads = logit_ref.shape[0]
    _, low, _ = bounds(len_ref, rows)
    low_ref[...] = jnp.full(low_ref.shape, low, jnp.int32)
    key = k_ref[...].astype(F32)
    own_ref[:rows, :dim] = (key * rms(key) * gain_ref[...]).astype(BF16)
    own_ref[:rows, dim:] = v_ref[...]
    log_gate = log_sigmoid(logit_ref[...].astype(F32))
    zero = jnp.zeros((TAIL - 3 * heads, rows), F32)
    parts = jnp.concatenate(list(split3(log_gate)) + [zero], axis=0).astype(BF16)

    def sums(test):
        result = dot_nn(parts, ones_where(rows, test))
        total = result[:heads] + result[heads : 2 * heads] + result[2 * heads : 3 * heads]
        return total

    onward = jnp.concatenate(list(split3(sums(lambda u, t: u >= t))) + [zero], axis=0)
    own_ref[rows:, :] = onward.astype(BF16)
    share_ref[...] = onward.astype(BF16)
    past = -sums(lambda u, t: u <= t)
    tail_ref[...] = jnp.concatenate(list(split3(past)) + [zero], axis=0).astype(BF16)


def key_columns(kaug, raw, tail, extra):
    rows = kaug.shape[0]
    dim = raw.shape[1] // 2
    kaug[:, :dim] = raw[:rows, :dim]
    zero = jnp.zeros((dim - 2 * TAIL, rows), F32)
    filled = jnp.concatenate([tail, extra.astype(F32), zero], axis=0)
    kaug[:, dim:] = filled.T.astype(BF16)


def strictly_after(tail):
    rows = tail.shape[1]
    moved = pltpu.roll(tail.astype(F32), rows - 1, 1)
    return jnp.where(iota(moved.shape, 1) == rows - 1, 0.0, moved)


def forward_block(kaug, qt, raw, tail, extra, kt, store, mixed, causal):
    rows = kaug.shape[0]
    dim = raw.shape[1] // 2
    key_columns(kaug, raw, tail, extra)
    both = flip(raw[:rows, :])
    kt[:dim, :] = both[:dim]
    kt[dim:, :] = ones_rows(rows)
    value_t = jnp.concatenate([both[dim:], ones_rows(rows)], axis=0)
    for part in chunks(qt.shape[1]):
        scores = dot_nn(kaug[...], qt[:, part])
        if causal:
            place = iota(scores.shape, 1)
            scores = jnp.where(iota(scores.shape, 0) <= place - place // rows * rows, scores, -BIG)
        store[:, part] = jnp.exp(scores).astype(BF16)
    for part in chunks(qt.shape[1]):
        mixed(part, dot_nn(value_t, store[:, part]))


def own_kernel(n, *refs):
    own_ref, tail_ref, qt, gt, acc, w_ref, kt, extra_ref, kaug = refs[4:13]
    fetch(refs[:4], refs[13:17], refs[17])
    len_ref, q_ref, g_ref, gain_ref = refs[13:17]
    rows = q_ref.shape[0]
    dim = gain_ref.shape[1]
    heads = q_ref.shape[1] // dim
    scale = dim ** (-0.5)
    me, _, spans = bounds(len_ref, rows)
    row = iota((TAIL, rows), 0)
    for k in range(n):
        tile = iota((TAIL, rows), 1) // TILE + (me ^ k) * (rows // TILE)
        extra = jnp.where(row < 3, 1.0, 0.0)
        for d, (start, end) in enumerate(spans):
            inside = jnp.where((tile >= start) & (tile < end), 1.0, 0.0)
            extra = jnp.where(row == 3 + d, inside, extra)
        extra_ref[k] = extra.astype(BF16)
    tail = tail_ref[...].astype(F32)
    past = -(tail[:heads] + tail[heads : 2 * heads] + tail[2 * heads : 3 * heads])
    parts = split3(past)
    docs = (row >= 3) & (row < 3 + len(spans))
    other = jnp.where(docs, (extra_ref[0].astype(F32) - 1.0) * BIG, 0.0)
    for h in range(heads):
        x = q_ref[:, cols(h, dim)].astype(F32)
        normed = x * rms(x) * (gain_ref[...] * scale)
        qt[:dim, cols(h, rows)] = flip(normed.astype(BF16))
        gt[:, cols(h, rows)] = flip(g_ref[:, cols(h, dim)])
        mine = (row < 3 * heads) & (row - row // heads * heads == h)
        qt[dim : dim + TAIL, cols(h, rows)] = jnp.where(mine, 1.0, 0.0).astype(BF16)
        gate = other
        for s in range(3):
            gate = jnp.where(row == s, parts[s][h : h + 1], gate)
        qt[dim + TAIL : dim + 2 * TAIL, cols(h, rows)] = gate.astype(BF16)
        qt[dim + 2 * TAIL :, cols(h, rows)] = jnp.zeros((dim - 2 * TAIL, rows), BF16)

    def mixed(part, value):
        acc[:, part] = value

    forward_block(kaug, qt, own_ref, tail, extra_ref[0], kt, w_ref, mixed, True)


def early_kernel(ks, low_ref, qt, extra_ref, *refs):
    raw_refs = refs[: len(ks)]
    w_ref, o_ref, kt_ref, kaug = refs[len(ks) :]
    rows = kaug.shape[0]
    me, low = first_block(low_ref)
    for i, k in enumerate(ks):
        raw = raw_refs[i]

        def mixed(part, value):
            o_ref[i, :, part] = value

        @pl.when(is_active(me, low, k))
        def _():
            tail = strictly_after(raw[rows:, :])
            forward_block(
                kaug, qt, raw, tail, extra_ref[k], kt_ref.at[i], w_ref.at[i], mixed, False
            )


def second_kernel(n, heads, before, ks, last, low_ref, qt, extra_ref, acc0, o_ref, share_ref, *refs):
    raw_refs = dict(zip([k for k in range(1, n) if k != last], refs[: n - 2]))
    w_ref, acc, kt_ref, between_ref, kaug = refs[n - 2 :]
    rows = kaug.shape[0]
    me, low = first_block(low_ref)
    wholes = {}
    for k in range(1, n):
        tail = share_ref[...] if k == last else raw_refs[k][rows:, :]
        tail = tail.astype(F32)
        total = tail[:heads] + tail[heads : 2 * heads] + tail[2 * heads : 3 * heads]
        wholes[k] = jnp.broadcast_to(total[:, :1], (heads, rows))
    for k in range(n):
        total = jnp.zeros((heads, rows), F32)
        for other in range(1, n):
            if other != k:
                b = me ^ other
                total = total + jnp.where((b > (me ^ k)) & (b < me), wholes[other], 0.0)
        between_ref[k] = lay_out(total)

    acc[...] = acc0[...]
    for i, k in enumerate(before):

        @pl.when(is_active(me, low, k))
        def _():
            root = jnp.exp(0.5 * between_ref[k])
            for part in chunks(root.shape[1]):
                acc[:, part] += o_ref[i, :, part] * root[:, part] * root[:, part]

    for i, k in enumerate(ks):

        @pl.when(is_active(me, low, k))
        def _():
            root = jnp.exp(0.5 * between_ref[k])

            def mixed(part, value):
                acc[:, part] += value * root[:, part] * root[:, part]

            raw = raw_refs[k]
            tail = strictly_after(raw[rows:, :])
            forward_block(
                kaug, qt, raw, tail, extra_ref[k], kt_ref.at[i], w_ref.at[i], mixed, False
            )


def backward_block(rows, raw, weights, factor, inner, kt, qt, gt, ds, plow, acc, kg, piece, gcol):
    dim = raw.shape[1] // 2
    for part in chunks(qt.shape[1]):
        grad = dot_nn(raw[:rows, dim:], gt[:, part])
        prob = weights[:, part].astype(F32) * factor[:, part]
        plow[:, part] = prob.astype(BF16)
        ds[:, part] = (prob * (grad - inner[:, part])).astype(BF16)
    for part in chunks(qt.shape[1]):
        acc[:, part] += dot_nn(kt[...], ds[:, part])
    key_part = dot_nt(qt[: dim + ONES, :], ds[...])
    piece[:dim, :] = key_part[:dim].astype(BF16)
    gcol[...] = -key_part[dim : dim + 8]
    kg[...] += key_part[:dim] * kt[:dim, :].astype(F32)
    piece[dim:, :] = dot_nt(gt[...], plow[...]).astype(BF16)


def idle_block(piece, gcol):
    piece[...] = jnp.zeros(piece.shape, BF16)
    gcol[...] = jnp.zeros(gcol.shape, F32)


def backward_set(ks, me, low, rows, raws, sources, between, log_ref, inner, state, pieces, gcols):
    qt, gt, ds, plow, acc, kg = state
    for i, k in enumerate(ks):
        weights, kt = sources[k]

        @pl.when(is_active(me, low, k))
        def _():
            factor = jnp.exp(between[k] - log_ref[...])
            backward_block(
                rows, raws[k], weights, factor, inner, kt, qt, gt, ds, plow, acc, kg,
                pieces[i], gcols[i],
            )

        if k:

            @pl.when(~is_active(me, low, k))
            def _():
                idle_block(pieces[i], gcols[i])


def source_map(ks_a, ks_b, last, arrays):
    wa, ka, wb, kb, wl, kl = arrays
    found = {k: (wa.at[i], ka.at[i]) for i, k in enumerate(ks_a)}
    found.update({k: (wb.at[i], kb.at[i]) for i, k in enumerate(ks_b)})
    found[last] = (wl, kl)
    return found


def middle_kernel(ks_a, ks_b, last, ks, heads, *refs):
    low_ref, qt, gt, extra_ref, acc0, between = refs[:6]
    stores = refs[6:10]
    raws = dict(zip([last] + ks, refs[10 : 11 + len(ks)]))
    refs = refs[11 + len(ks) :]
    mixed_ref, acc, log_ref, inner, kg, w_last, kt_last = refs[:7]
    gcols = [refs[7].at[i] for i in range(len(ks))]
    rows = qt.shape[1] // heads
    pieces = [refs[8].at[cols(i, rows)] for i in range(len(ks))]
    kaug, ds, plow = refs[9:]
    dim = gt.shape[0]
    me, low = first_block(low_ref)
    acc[...] = acc0[...]

    @pl.when(is_active(me, low, last))
    def _():
        root = jnp.exp(0.5 * between[last])

        def mixed(part, value):
            acc[:, part] += value * root[:, part] * root[:, part]

        raw = raws[last]
        tail = strictly_after(raw[rows:, :])
        forward_block(kaug, qt, raw, tail, extra_ref[last], kt_last, w_last, mixed, False)

    for part in chunks(qt.shape[1]):
        total = acc[dim : dim + 1, part]
        mixed_t = (acc[:dim, part] * (1.0 / total)).astype(BF16)
        mixed_ref[:, part] = mixed_t
        log_ref[:, part] = jnp.log(total)
        product = gt[:, part].astype(F32) * mixed_t.astype(F32)
        inner[:, part] = jnp.sum(product, axis=0, keepdims=True)
    acc[...] = jnp.zeros(acc.shape, F32)
    kg[...] = jnp.zeros(kg.shape, F32)
    sources = source_map(ks_a, ks_b, last, stores + (w_last, kt_last))
    state = (qt, gt, ds, plow, acc, kg)
    backward_set(ks, me, low, rows, raws, sources, between, log_ref, inner, state, pieces, gcols)


def middle_two_kernel(ks_a, ks_b, last, ks, heads, *refs):
    low_ref, qt, gt, acc0, between, log_ref, inner, kg0 = refs[:8]
    sources = source_map(ks_a, ks_b, last, refs[8:14])
    raws = dict(zip(ks, refs[14 : 14 + len(ks)]))
    refs = refs[14 + len(ks) :]
    acc, kg = refs[:2]
    gcols = [refs[2].at[i] for i in range(len(ks))]
    rows = qt.shape[1] // heads
    pieces = [refs[3].at[cols(i, rows)] for i in range(len(ks))]
    ds, plow = refs[4:]
    me, low = first_block(low_ref)
    acc[...] = acc0[...]
    kg[...] = kg0[...]
    state = (qt, gt, ds, plow, acc, kg)
    backward_set(ks, me, low, rows, raws, sources, between, log_ref, inner, state, pieces, gcols)


def late_kernel(n, ks_a, ks_b, odds, low_ref, kgain_ref, qgain_ref, *refs):
    half = n // 2
    qt, gt, acc0, between, log_ref, inner, kg0 = refs[:7]
    sources = source_map(ks_a, ks_b, 0, refs[7:13])
    g_odds = refs[13 : 13 + len(odds)]
    refs = refs[13 + len(odds) :]
    raws = {2 * s: refs[s] for s in range(half)}
    acc, keep_ref, give_ref = refs[half : half + 3]
    piece_refs = refs[half + 3 : 2 * half + 3]
    kg, ds, plow, gall = refs[2 * half + 3 :]
    rows = ds.shape[0]
    dim = qgain_ref.shape[1]
    heads = qt.shape[1] // rows
    me, low = first_block(low_ref)
    acc[...] = acc0[...]
    kg[...] = kg0[...]
    for ks, g_odd in zip(odds, g_odds):
        for i, k in enumerate(ks):
            gall[k] = g_odd[i]
    ks = [2 * s for s in range(half - 1, -1, -1)]
    pieces = [piece_refs[k // 2] for k in ks]
    gcols = [gall.at[k] for k in ks]
    state = (qt, gt, ds, plow, acc, kg)
    backward_set(ks, me, low, rows, raws, sources, between, log_ref, inner, state, pieces, gcols)

    qg = jnp.zeros((dim, rows), F32)
    row_sums = []
    for h in range(heads):
        part = cols(h, rows)
        qg = qg + acc[:dim, part] * qt[:dim, part].astype(F32)
        row_sums.append(acc[dim : dim + 1, part])
    gall[0] += jnp.concatenate(row_sums + row_sums, axis=0)[:8]
    query_gain = jnp.sum(qg.T, axis=0, keepdims=True) / qgain_ref[...]
    key_gain = jnp.sum(kg[...].T, axis=0, keepdims=True) / kgain_ref[...]
    gain_row = jnp.concatenate([query_gain, key_gain], axis=1)
    is_gain = iota((8, rows), 0) == heads
    later = ones_where(rows, lambda u, t: u >= t)
    stacked = jnp.concatenate([gall[k] for k in range(n)], axis=0)
    suffix = sum(dot_nn(part.astype(BF16), later) for part in split3(stacked))
    locals_ = [suffix[8 * k : 8 * k + 8] for k in range(n)]
    wholes = [jnp.broadcast_to(local[:, :1], (8, rows)) for local in locals_]
    results = []
    for k in range(n):
        total = locals_[k]
        for other in range(n):
            if other != k:
                total = total + jnp.where((me ^ other) > (me ^ k), wholes[other], 0.0)
        total = jnp.where(is_active(me, low, k), total, 0.0)
        results.append(jnp.where(is_gain, gain_row, total))
    for s in range(half):
        keep_ref[8 * s : 8 * s + 8, :] = results[2 * s]
        give_ref[8 * s : 8 * s + 8, :] = results[2 * s + 1]


def query_kernel(q_ref, qgain_ref, acc, mixed_ref, qgrad_ref, out_ref):
    rows = q_ref.shape[0]
    dim = qgain_ref.shape[1]
    scale = dim ** (-0.5)
    eye = ones_where(rows, lambda i, j: i == j)
    for h in range(q_ref.shape[1] // dim):
        out_ref[:, cols(h, dim)] = dot_nt(eye, mixed_ref[:, cols(h, rows)]).astype(BF16)
        x = q_ref[:, cols(h, dim)].astype(F32)
        rstd = rms(x)
        hat = x * rstd
        back = acc[:dim, cols(h, rows)].T.astype(BF16).astype(F32) * (qgain_ref[...] * scale)
        mean = jnp.mean(back * hat, axis=-1, keepdims=True)
        qgrad_ref[:, cols(h, dim)] = (rstd * (back - hat * mean)).astype(BF16)


def add_kernel(at, a_ref, b_ref, o_ref):
    other = b_ref[cols(at, a_ref.shape[0]), :]
    o_ref[...] = (a_ref[...].astype(F32) + other.astype(F32)).astype(BF16)


def settle_kernel(heads, keep_ref, got_ref, total_ref, gain_ref):
    total_ref[...] = keep_ref[...] + got_ref[...]
    gain_ref[...] = total_ref[heads : heads + 1, :]


def pair_kernel(a_ref, b_ref, o_ref):
    o_ref[...] = a_ref[...] + b_ref[...]


def spread_kernel(heads, total_ref, a_ref, b_ref, *outs):
    gain = a_ref[...] + b_ref[...]
    for s, out in enumerate(outs):
        rows = total_ref[8 * s : 8 * s + 8, :]
        out[...] = jnp.where(iota(rows.shape, 0) == heads, gain, rows)


def finish_kernel(at, k_ref, gain_ref, *refs):
    piece_refs = refs[:-2]
    kgrad_ref, vgrad_ref = refs[-2:]
    dim = k_ref.shape[1]
    rows = k_ref.shape[0]
    total = piece_refs[0][...].astype(F32) + piece_refs[1][at * rows :, :].astype(F32)
    for ref in piece_refs[2:]:
        total = total + ref[...].astype(F32)
    vgrad_ref[...] = total[dim:].T.astype(BF16)
    x = k_ref[...].astype(F32)
    rstd = rms(x)
    hat = x * rstd
    back = total[:dim].T * gain_ref[...]
    mean = jnp.mean(back * hat, axis=-1, keepdims=True)
    kgrad_ref[...] = (rstd * (back - hat * mean)).astype(BF16)


def forget_kernel(logit_ref, *refs):
    small_refs = refs[:-2]
    fgrad_ref, gains_ref = refs[-2:]
    heads = logit_ref.shape[0]
    small = small_refs[0][...]
    for ref in small_refs[1:]:
        small = small + ref[...]
    logit = logit_ref[...].astype(F32)
    fgrad_ref[...] = small[:heads] * (1.0 / (1.0 + jnp.exp(logit)))
    row = small[heads : heads + 1]
    dim = row.shape[1] // 2
    gains_ref[...] = jnp.concatenate([row[:, :dim], row[:, dim:]], axis=0)


def whole_step(queries, key_vectors, values, forget_logit, out_grad, query_gain, key_gain, lengths):
    n = lax.axis_size("seq")
    half = n // 2
    rows, full = queries.shape[1:]
    dim = query_gain.shape[0]
    heads = full // dim
    wide = heads * rows
    width = 2 * dim
    tall = dim + ONES
    query, grad, key, logit = queries[0], out_grad[0], key_vectors[0], forget_logit[0]
    qgain, kgain = query_gain[None], key_gain[None]
    matmul = 2 * rows * wide * width
    head_row = struct(heads, rows, dtype=F32)
    line = struct(1, wide, dtype=F32)
    state = struct(tall, wide, dtype=F32)
    key_sum = struct(dim, rows, dtype=F32)
    piece = struct(rows, width)
    wide_scratch = pltpu.VMEM((rows, wide), BF16)

    inputs = [lengths, key, values[0], logit, kgain]
    own, share, own_tail, low = kernel_call(
        pack_kernel, inputs,
        (
            struct(rows + TAIL, width), struct(TAIL, rows), struct(TAIL, rows),
            struct(8, 128, dtype=jnp.int32),
        ),
        near(inputs), far=5,
    )
    gather_order = [2] + list(range(n - 2, 2, -2))
    last = gather_order[-1] + 1
    blocks = {0: own}
    for k in gather_order:
        blocks[k] = swap(own, "seq", k)
    blocks[1] = swap(own, "seq", 1)
    share = swap(share, "seq", last)
    for k in gather_order:
        blocks[k + 1] = swap(blocks[k], "seq", 1)

    inputs = [lengths, query, grad, qgain]
    kaug_scratch = pltpu.VMEM((rows, width), BF16)
    qt, gt, acc, w0, kt0, extra = kernel_call(
        functools.partial(own_kernel, n), inputs + [own, own_tail],
        (
            struct(width, wide), struct(dim, wide), state, struct(rows, wide), struct(tall, rows),
            struct(n, TAIL, rows),
        ),
        [kaug_scratch] + near(inputs),
        flops=2 * matmul, far=4,
    )

    def stores(count):
        return struct(count, rows, wide), struct(count, tall, rows)

    ks_a = [1] + gather_order[:-1]
    ks_b = [gather_order[-1]] + [k + 1 for k in gather_order[:-1]]
    w_a, o_a, kt_a = kernel_call(
        functools.partial(early_kernel, ks_a),
        [low, qt, extra] + [blocks[k] for k in ks_a],
        (stores(half)[0], struct(half, tall, wide, dtype=F32), stores(half)[1]),
        [kaug_scratch],
        flops=2 * half * matmul,
    )
    w_b, acc, kt_b, between = kernel_call(
        functools.partial(second_kernel, n, heads, ks_a, ks_b, last),
        [low, qt, extra, acc, o_a, share] + [blocks[k] for k in range(1, n) if k != last],
        (stores(half - 1)[0], state, stores(half - 1)[1], struct(n, 1, wide, dtype=F32)),
        [kaug_scratch],
        flops=2 * half * matmul,
    )
    down = list(range(n - 1, 0, -2))
    odds = [down[: half // 2], down[half // 2 :]]
    kept = [w_a, kt_a, w_b, kt_b]
    results = kernel_call(
        functools.partial(middle_kernel, ks_a, ks_b, last, odds[0], heads),
        [low, qt, gt, extra, acc, between] + kept + [blocks[k] for k in [last] + odds[0]],
        (
            struct(dim, wide), state, line, line, key_sum, struct(rows, wide), struct(tall, rows),
            struct(len(odds[0]), 8, rows, dtype=F32), struct(len(odds[0]) * rows, width),
        ),
        [kaug_scratch, wide_scratch, wide_scratch],
        flops=4 * half * matmul,
    )
    mixed_t, acc, log_total, inner, key_acc, w_last, kt_last, gate_one, stack = results
    stacks = [swap(stack, "seq", 1)]
    results = kernel_call(
        functools.partial(middle_two_kernel, ks_a, ks_b, last, odds[1], heads),
        [low, qt, gt, acc, between, log_total, inner, key_acc] + kept + [w_last, kt_last]
        + [blocks[k] for k in odds[1]],
        (
            state, key_sum, struct(len(odds[1]), 8, rows, dtype=F32),
            struct(len(odds[1]) * rows, width),
        ),
        [wide_scratch, wide_scratch],
        flops=2 * half * matmul,
    )
    acc, key_acc, gate_two, stack = results
    stacks.append(swap(stack, "seq", 1))
    place = {k: (g, i) for g, ks in enumerate(odds) for i, k in enumerate(ks)}

    small = struct(8 * half, rows, dtype=F32)
    results = kernel_call(
        functools.partial(late_kernel, n, ks_a, ks_b, odds),
        [low, kgain, qgain, qt, gt, acc, between, log_total, inner, key_acc]
        + kept + [w0, kt0, gate_one, gate_two]
        + [blocks[2 * s] for s in range(half)],
        (state, small, small) + (piece,) * half,
        [pltpu.VMEM((dim, rows), F32), wide_scratch, wide_scratch, pltpu.VMEM((n, 8, rows), F32)],
        flops=4 * half * matmul,
    )
    acc, keep, give = results[:3]
    even = results[3:]

    got = swap(give, "seq", 1)
    query_grad, attention = kernel_call(
        query_kernel, [query, qgain, acc, mixed_t],
        (struct(rows, full), struct(rows, full)), flops=matmul,
    )
    arrived = [even[0], stacks[1]]
    for s in range(half - 1, 0, -1):
        group, at = place[2 * s + 1]
        both = kernel_call(functools.partial(add_kernel, at), [even[s], stacks[group]], piece)
        arrived.append(swap(both, "seq", 2 * s))
    eight = struct(8, rows, dtype=F32)
    gain_line = struct(1, width, dtype=F32)
    total, gain = kernel_call(
        functools.partial(settle_kernel, heads), [keep, got], (small, gain_line)
    )
    bit = 1
    while 2 * bit < lax.axis_size("rep"):
        gain = kernel_call(pair_kernel, [gain, swap(gain, "rep", bit)], gain_line)
        bit *= 2
    smalls = kernel_call(
        functools.partial(spread_kernel, heads),
        [total, gain, swap(gain, "rep", bit)], (eight,) * half,
    )
    smalls = [smalls[0]] + [swap(smalls[s], "seq", 2 * s) for s in range(1, half)]
    forget_grad, gains = kernel_call(
        forget_kernel, [logit] + smalls, (head_row, struct(2, dim, dtype=F32))
    )
    key_grad, value_grad = kernel_call(
        functools.partial(finish_kernel, place[1][1]), [key, kgain] + arrived, (struct(rows, dim), struct(rows, dim)),
        flops=matmul,
    )
    return (
        attention[None],
        query_grad[None],
        key_grad[None],
        value_grad[None],
        forget_grad[None],
        gains,
    )


def solution(mesh):
    return jax.shard_map(
        whole_step,
        mesh=mesh,
        in_specs=(
            P("rep", "seq", None),
            P("rep", "seq", None),
            P("rep", "seq", None),
            P("rep", None, "seq"),
            P("rep", "seq", None),
            P(),
            P(),
            P("rep", None),
        ),
        out_specs=(
            P("rep", "seq", None),
            P("rep", "seq", None),
            P("rep", "seq", None),
            P("rep", "seq", None),
            P("rep", None, "seq"),
            P(),
        ),
        check_vma=False,
    )
```

```python
import functools

import jax
import jax.numpy as jnp
from jax import lax
from jax.experimental import pallas as pl
from jax.experimental.pallas import tpu as pltpu
from jax.sharding import PartitionSpec as P


TILE = 64
EPS = 1e-06
TAIL = 16
ONES = 16
CHUNK = 512
BIG = 1e30
F32 = jnp.float32
BF16 = jnp.bfloat16
VMEM = pl.BlockSpec(memory_space=pltpu.VMEM)
HBM = pl.BlockSpec(memory_space=pltpu.HBM)


def swap(value, axis, bit):
    count = lax.axis_size(axis)
    return lax.ppermute(value, axis, [(i, i ^ bit) for i in range(count)])


def struct(*shape, dtype=BF16):
    return jax.ShapeDtypeStruct(shape, dtype)


def kernel_call(kernel, operands, outs, scratch=(), limit=8 << 20, flops=1 << 20, far=0):
    in_specs = [HBM] * far + [VMEM] * (len(operands) - far)
    operands = [
        pltpu.with_memory_space_constraint(x, pltpu.HBM) if i < far else x
        for i, x in enumerate(operands)
    ]
    return pl.pallas_call(
        kernel,
        out_shape=outs,
        in_specs=in_specs,
        out_specs=jax.tree.map(lambda _: VMEM, outs),
        scratch_shapes=list(scratch),
        compiler_params=pltpu.CompilerParams(vmem_limit_bytes=limit),
        cost_estimate=pl.CostEstimate(flops=flops, bytes_accessed=1 << 20, transcendentals=0),
    )(*operands)


def dot_nn(a, b):
    return lax.dot_general(a, b, (((1,), (0,)), ((), ())), preferred_element_type=F32)


def dot_nt(a, b):
    return lax.dot_general(a, b, (((1,), (1,)), ((), ())), preferred_element_type=F32)


def iota(shape, axis):
    return lax.broadcasted_iota(jnp.int32, shape, axis)


def split3(x):
    hi = x.astype(BF16).astype(F32)
    rest = x - hi
    mid = rest.astype(BF16).astype(F32)
    return hi, mid, rest - mid


def rms(x):
    return lax.rsqrt(jnp.mean(x * x, axis=-1, keepdims=True) + EPS)


def flip(block):
    return block.astype(F32).T.astype(BF16)


def ones_where(count, test):
    shape = (count, count)
    return jnp.where(test(iota(shape, 0), iota(shape, 1)), 1.0, 0.0).astype(BF16)


def ones_rows(count):
    return jnp.where(iota((ONES, count), 0) == 0, 1.0, 0.0).astype(BF16)


def cols(h, rows):
    return slice(h * rows, (h + 1) * rows)


def chunks(wide):
    step = min(wide, CHUNK)
    return [slice(at, at + step) for at in range(0, wide, step)]


def lay_out(per_head):
    return jnp.concatenate([per_head[h : h + 1] for h in range(per_head.shape[0])], axis=1)


def log_sigmoid(x):
    small = jnp.exp(-jnp.abs(x))
    series = small * (1.0 - small * (0.5 - small * (1.0 / 3.0 - small * 0.25)))
    return jnp.minimum(x, 0.0) - jnp.where(small < 0.01, series, jnp.log(1.0 + small))


def bounds(len_ref, rows):
    me = lax.axis_index("seq")
    tiles = rows // TILE
    spans = []
    start = jnp.int32(0)
    begin = jnp.int32(0)
    for d in range(len_ref.shape[1]):
        end = start + len_ref[0, d]
        spans.append((start, end))
        begin = jnp.where(start <= me * tiles, start, begin)
        start = end
    return me, begin // tiles, spans


def first_block(low_ref):
    return lax.axis_index("seq"), low_ref[0, 0]


def is_active(me, low, k):
    b = me ^ k
    return (b <= me) & (b >= low)


def fetch(sources, targets, sem):
    copies = [pltpu.make_async_copy(*pair, sem.at[i]) for i, pair in enumerate(zip(sources, targets))]
    for copy in copies:
        copy.start()
    for copy in copies:
        copy.wait()


def near(operands):
    spaces = [pltpu.SMEM if x.dtype == jnp.int32 else pltpu.VMEM for x in operands]
    return [space(x.shape, x.dtype) for space, x in zip(spaces, operands)] + [
        pltpu.SemaphoreType.DMA((len(operands),))
    ]


def pack_kernel(*refs):
    own_ref, share_ref, tail_ref, low_ref = refs[5:9]
    fetch(refs[:5], refs[9:14], refs[14])
    len_ref, k_ref, v_ref, logit_ref, gain_ref = refs[9:14]
    rows, dim = k_ref.shape
    heads = logit_ref.shape[0]
    _, low, _ = bounds(len_ref, rows)
    low_ref[...] = jnp.full(low_ref.shape, low, jnp.int32)
    key = k_ref[...].astype(F32)
    own_ref[:rows, :dim] = (key * rms(key) * gain_ref[...]).astype(BF16)
    own_ref[:rows, dim:] = v_ref[...]
    log_gate = log_sigmoid(logit_ref[...].astype(F32))
    zero = jnp.zeros((TAIL - 3 * heads, rows), F32)
    parts = jnp.concatenate(list(split3(log_gate)) + [zero], axis=0).astype(BF16)

    def sums(test):
        result = dot_nn(parts, ones_where(rows, test))
        total = result[:heads] + result[heads : 2 * heads] + result[2 * heads : 3 * heads]
        return total

    onward = jnp.concatenate(list(split3(sums(lambda u, t: u >= t))) + [zero], axis=0)
    own_ref[rows:, :] = onward.astype(BF16)
    share_ref[...] = onward.astype(BF16)
    past = -sums(lambda u, t: u <= t)
    tail_ref[...] = jnp.concatenate(list(split3(past)) + [zero], axis=0).astype(BF16)


def key_columns(kaug, raw, tail, extra):
    rows = kaug.shape[0]
    dim = raw.shape[1] // 2
    kaug[:, :dim] = raw[:rows, :dim]
    zero = jnp.zeros((dim - 2 * TAIL, rows), F32)
    filled = jnp.concatenate([tail, extra.astype(F32), zero], axis=0)
    kaug[:, dim:] = filled.T.astype(BF16)


def strictly_after(tail):
    rows = tail.shape[1]
    moved = pltpu.roll(tail.astype(F32), rows - 1, 1)
    return jnp.where(iota(moved.shape, 1) == rows - 1, 0.0, moved)


def forward_block(kaug, qt, raw, tail, extra, kt, store, mixed, causal):
    rows = kaug.shape[0]
    dim = raw.shape[1] // 2
    key_columns(kaug, raw, tail, extra)
    both = flip(raw[:rows, :])
    kt[:dim, :] = both[:dim]
    kt[dim:, :] = ones_rows(rows)
    value_t = jnp.concatenate([both[dim:], ones_rows(rows)], axis=0)
    for part in chunks(qt.shape[1]):
        scores = dot_nn(kaug[...], qt[:, part])
        if causal:
            place = iota(scores.shape, 1)
            scores = jnp.where(iota(scores.shape, 0) <= place - place // rows * rows, scores, -BIG)
        store[:, part] = jnp.exp(scores).astype(BF16)
    for part in chunks(qt.shape[1]):
        mixed(part, dot_nn(value_t, store[:, part]))


def own_kernel(n, *refs):
    own_ref, tail_ref, qt, gt, acc, w_ref, kt, extra_ref, kaug = refs[4:13]
    fetch(refs[:4], refs[13:17], refs[17])
    len_ref, q_ref, g_ref, gain_ref = refs[13:17]
    rows = q_ref.shape[0]
    dim = gain_ref.shape[1]
    heads = q_ref.shape[1] // dim
    scale = dim ** (-0.5)
    me, _, spans = bounds(len_ref, rows)
    row = iota((TAIL, rows), 0)
    for k in range(n):
        tile = iota((TAIL, rows), 1) // TILE + (me ^ k) * (rows // TILE)
        extra = jnp.where(row < 3, 1.0, 0.0)
        for d, (start, end) in enumerate(spans):
            inside = jnp.where((tile >= start) & (tile < end), 1.0, 0.0)
            extra = jnp.where(row == 3 + d, inside, extra)
        extra_ref[k] = extra.astype(BF16)
    tail = tail_ref[...].astype(F32)
    past = -(tail[:heads] + tail[heads : 2 * heads] + tail[2 * heads : 3 * heads])
    parts = split3(past)
    docs = (row >= 3) & (row < 3 + len(spans))
    other = jnp.where(docs, (extra_ref[0].astype(F32) - 1.0) * BIG, 0.0)
    for h in range(heads):
        x = q_ref[:, cols(h, dim)].astype(F32)
        normed = x * rms(x) * (gain_ref[...] * scale)
        qt[:dim, cols(h, rows)] = flip(normed.astype(BF16))
        gt[:, cols(h, rows)] = flip(g_ref[:, cols(h, dim)])
        mine = (row < 3 * heads) & (row - row // heads * heads == h)
        qt[dim : dim + TAIL, cols(h, rows)] = jnp.where(mine, 1.0, 0.0).astype(BF16)
        gate = other
        for s in range(3):
            gate = jnp.where(row == s, parts[s][h : h + 1], gate)
        qt[dim + TAIL : dim + 2 * TAIL, cols(h, rows)] = gate.astype(BF16)
        qt[dim + 2 * TAIL :, cols(h, rows)] = jnp.zeros((dim - 2 * TAIL, rows), BF16)

    def mixed(part, value):
        acc[:, part] = value

    forward_block(kaug, qt, own_ref, tail, extra_ref[0], kt, w_ref, mixed, True)


def early_kernel(ks, low_ref, qt, extra_ref, *refs):
    raw_refs = refs[: len(ks)]
    w_ref, o_ref, kt_ref, kaug = refs[len(ks) :]
    rows = kaug.shape[0]
    me, low = first_block(low_ref)
    for i, k in enumerate(ks):
        raw = raw_refs[i]

        def mixed(part, value):
            o_ref[i, :, part] = value

        @pl.when(is_active(me, low, k))
        def _():
            tail = strictly_after(raw[rows:, :])
            forward_block(
                kaug, qt, raw, tail, extra_ref[k], kt_ref.at[i], w_ref.at[i], mixed, False
            )

        @pl.when(jnp.logical_not(is_active(me, low, k)))
        def _():
            clear(kt_ref.at[i], w_ref.at[i])


def second_kernel(n, heads, before, ks, last, low_ref, qt, extra_ref, acc0, o_ref, share_ref, *refs):
    raw_refs = dict(zip([k for k in range(1, n) if k != last], refs[: n - 2]))
    w_ref, acc, kt_ref, between_ref, kaug = refs[n - 2 :]
    rows = kaug.shape[0]
    me, low = first_block(low_ref)
    wholes = {}
    for k in range(1, n):
        tail = share_ref[...] if k == last else raw_refs[k][rows:, :]
        tail = tail.astype(F32)
        total = tail[:heads] + tail[heads : 2 * heads] + tail[2 * heads : 3 * heads]
        wholes[k] = jnp.broadcast_to(total[:, :1], (heads, rows))
    for k in range(n):
        total = jnp.zeros((heads, rows), F32)
        for other in range(1, n):
            if other != k:
                b = me ^ other
                total = total + jnp.where((b > (me ^ k)) & (b < me), wholes[other], 0.0)
        between_ref[k] = lay_out(total)

    acc[...] = acc0[...]
    for i, k in enumerate(before):

        @pl.when(is_active(me, low, k))
        def _():
            root = jnp.exp(0.5 * between_ref[k])
            for part in chunks(root.shape[1]):
                acc[:, part] += o_ref[i, :, part] * root[:, part] * root[:, part]

    for i, k in enumerate(ks):

        @pl.when(is_active(me, low, k))
        def _():
            root = jnp.exp(0.5 * between_ref[k])

            def mixed(part, value):
                acc[:, part] += value * root[:, part] * root[:, part]

            raw = raw_refs[k]
            tail = strictly_after(raw[rows:, :])
            forward_block(
                kaug, qt, raw, tail, extra_ref[k], kt_ref.at[i], w_ref.at[i], mixed, False
            )

        @pl.when(jnp.logical_not(is_active(me, low, k)))
        def _():
            clear(kt_ref.at[i], w_ref.at[i])


def backward_blocks(rows, items, inner, qt, gt, ds, plow, acc, kg):
    dim = gt.shape[0]
    for i, (raw, weights, factor, kt, piece, gcol) in enumerate(items):
        for part in chunks(qt.shape[1]):
            grad = dot_nn(raw[:rows, dim:], gt[:, part])
            prob = weights[:, part].astype(F32) * factor[:, part]
            plow[i, :, part] = prob.astype(BF16)
            ds[i, :, part] = (prob * (grad - inner[:, part])).astype(BF16)
    for part in chunks(qt.shape[1]):
        acc[:, part] += sum(dot_nn(item[3][...], ds[i, :, part]) for i, item in enumerate(items))
    total = kg[...]
    for i, (raw, weights, factor, kt, piece, gcol) in enumerate(items):
        key_part = dot_nt(qt[: dim + ONES, :], ds[i])
        piece[:dim, :] = key_part[:dim].astype(BF16)
        gcol[...] = -key_part[dim : dim + 8]
        total = total + key_part[:dim] * kt[:dim, :].astype(F32)
        piece[dim:, :] = dot_nt(gt[...], plow[i]).astype(BF16)
    kg[...] = total


def clear(*targets):
    for ref in targets:
        ref[...] = jnp.zeros(ref.shape, ref.dtype)


def idle_block(piece, gcol):
    piece[...] = jnp.zeros(piece.shape, BF16)
    gcol[...] = jnp.zeros(gcol.shape, F32)


def backward_set(ks, me, low, rows, raws, sources, between, log_ref, inner, state, pieces, gcols):
    qt, gt, ds, plow, acc, kg = state
    for at in range(0, len(ks), 2):
        group = list(range(at, min(at + 2, len(ks))))
        needed = functools.reduce(jnp.logical_or, [is_active(me, low, ks[i]) for i in group])

        @pl.when(needed)
        def _():
            items = []
            for i in group:
                weights, kt = sources[ks[i]]
                factor = jnp.exp(between[ks[i]] - log_ref[...])
                items.append((raws[ks[i]], weights, factor, kt, pieces[i], gcols[i]))
            backward_blocks(rows, items, inner, qt, gt, ds, plow, acc, kg)

        @pl.when(jnp.logical_not(needed))
        def _():
            for i in group:
                idle_block(pieces[i], gcols[i])


def source_map(ks_a, ks_b, last, arrays):
    wa, ka, wb, kb, wl, kl = arrays
    found = {k: (wa.at[i], ka.at[i]) for i, k in enumerate(ks_a)}
    found.update({k: (wb.at[i], kb.at[i]) for i, k in enumerate(ks_b)})
    found[last] = (wl, kl)
    return found


def middle_kernel(ks_a, ks_b, last, ks, heads, *refs):
    low_ref, qt, gt, extra_ref, acc0, between = refs[:6]
    stores = refs[6:10]
    raws = dict(zip([last] + ks, refs[10 : 11 + len(ks)]))
    refs = refs[11 + len(ks) :]
    mixed_ref, acc, log_ref, inner, kg, w_last, kt_last = refs[:7]
    gcols = [refs[7].at[i] for i in range(len(ks))]
    rows = qt.shape[1] // heads
    pieces = [refs[8].at[cols(i, rows)] for i in range(len(ks))]
    kaug, ds, plow = refs[9:]
    dim = gt.shape[0]
    me, low = first_block(low_ref)
    acc[...] = acc0[...]

    @pl.when(is_active(me, low, last))
    def _():
        root = jnp.exp(0.5 * between[last])

        def mixed(part, value):
            acc[:, part] += value * root[:, part] * root[:, part]

        raw = raws[last]
        tail = strictly_after(raw[rows:, :])
        forward_block(kaug, qt, raw, tail, extra_ref[last], kt_last, w_last, mixed, False)

    @pl.when(jnp.logical_not(is_active(me, low, last)))
    def _():
        clear(kt_last, w_last)

    for part in chunks(qt.shape[1]):
        total = acc[dim : dim + 1, part]
        mixed_t = (acc[:dim, part] * (1.0 / total)).astype(BF16)
        mixed_ref[:, part] = mixed_t
        log_ref[:, part] = jnp.log(total)
        product = gt[:, part].astype(F32) * mixed_t.astype(F32)
        inner[:, part] = jnp.sum(product, axis=0, keepdims=True)
    acc[...] = jnp.zeros(acc.shape, F32)
    kg[...] = jnp.zeros(kg.shape, F32)
    sources = source_map(ks_a, ks_b, last, stores + (w_last, kt_last))
    state = (qt, gt, ds, plow, acc, kg)
    backward_set(ks, me, low, rows, raws, sources, between, log_ref, inner, state, pieces, gcols)


def middle_two_kernel(ks_a, ks_b, last, ks, heads, *refs):
    low_ref, qt, gt, acc0, between, log_ref, inner, kg0 = refs[:8]
    sources = source_map(ks_a, ks_b, last, refs[8:14])
    raws = dict(zip(ks, refs[14 : 14 + len(ks)]))
    refs = refs[14 + len(ks) :]
    acc, kg = refs[:2]
    gcols = [refs[2].at[i] for i in range(len(ks))]
    rows = qt.shape[1] // heads
    pieces = [refs[3].at[cols(i, rows)] for i in range(len(ks))]
    ds, plow = refs[4:]
    me, low = first_block(low_ref)
    acc[...] = acc0[...]
    kg[...] = kg0[...]
    state = (qt, gt, ds, plow, acc, kg)
    backward_set(ks, me, low, rows, raws, sources, between, log_ref, inner, state, pieces, gcols)


def late_kernel(n, ks_a, ks_b, odds, low_ref, kgain_ref, qgain_ref, *refs):
    half = n // 2
    qt, gt, acc0, between, log_ref, inner, kg0 = refs[:7]
    sources = source_map(ks_a, ks_b, 0, refs[7:13])
    g_odds = refs[13 : 13 + len(odds)]
    refs = refs[13 + len(odds) :]
    raws = {2 * s: refs[s] for s in range(half)}
    acc, keep_ref, give_ref = refs[half : half + 3]
    piece_refs = refs[half + 3 : 2 * half + 3]
    kg, ds, plow, gall = refs[2 * half + 3 :]
    rows = ds.shape[1]
    dim = qgain_ref.shape[1]
    heads = qt.shape[1] // rows
    me, low = first_block(low_ref)
    acc[...] = acc0[...]
    kg[...] = kg0[...]
    for ks, g_odd in zip(odds, g_odds):
        for i, k in enumerate(ks):
            gall[k] = g_odd[i]
    ks = [2 * s for s in range(half - 1, -1, -1)]
    pieces = [piece_refs[k // 2] for k in ks]
    gcols = [gall.at[k] for k in ks]
    state = (qt, gt, ds, plow, acc, kg)
    backward_set(ks, me, low, rows, raws, sources, between, log_ref, inner, state, pieces, gcols)

    qg = jnp.zeros((dim, rows), F32)
    row_sums = []
    for h in range(heads):
        part = cols(h, rows)
        qg = qg + acc[:dim, part] * qt[:dim, part].astype(F32)
        row_sums.append(acc[dim : dim + 1, part])
    gall[0] += jnp.concatenate(row_sums + row_sums, axis=0)[:8]
    query_gain = jnp.sum(qg.T, axis=0, keepdims=True) / qgain_ref[...]
    key_gain = jnp.sum(kg[...].T, axis=0, keepdims=True) / kgain_ref[...]
    gain_row = jnp.concatenate([query_gain, key_gain], axis=1)
    is_gain = iota((8, rows), 0) == heads
    later = ones_where(rows, lambda u, t: u >= t)
    stacked = jnp.concatenate([gall[k] for k in range(n)], axis=0)
    suffix = sum(dot_nn(part.astype(BF16), later) for part in split3(stacked))
    locals_ = [suffix[8 * k : 8 * k + 8] for k in range(n)]
    wholes = [jnp.broadcast_to(local[:, :1], (8, rows)) for local in locals_]
    results = []
    for k in range(n):
        total = locals_[k]
        for other in range(n):
            if other != k:
                total = total + jnp.where((me ^ other) > (me ^ k), wholes[other], 0.0)
        total = jnp.where(is_active(me, low, k), total, 0.0)
        results.append(jnp.where(is_gain, gain_row, total))
    for s in range(half):
        keep_ref[8 * s : 8 * s + 8, :] = results[2 * s]
        give_ref[8 * s : 8 * s + 8, :] = results[2 * s + 1]


def query_kernel(q_ref, qgain_ref, acc, mixed_ref, qgrad_ref, out_ref):
    rows = q_ref.shape[0]
    dim = qgain_ref.shape[1]
    scale = dim ** (-0.5)
    eye = ones_where(rows, lambda i, j: i == j)
    for h in range(q_ref.shape[1] // dim):
        out_ref[:, cols(h, dim)] = dot_nt(eye, mixed_ref[:, cols(h, rows)]).astype(BF16)
        x = q_ref[:, cols(h, dim)].astype(F32)
        rstd = rms(x)
        hat = x * rstd
        back = acc[:dim, cols(h, rows)].T.astype(BF16).astype(F32) * (qgain_ref[...] * scale)
        mean = jnp.mean(back * hat, axis=-1, keepdims=True)
        qgrad_ref[:, cols(h, dim)] = (rstd * (back - hat * mean)).astype(BF16)


def add_kernel(at, a_ref, b_ref, o_ref):
    other = b_ref[cols(at, a_ref.shape[0]), :]
    o_ref[...] = (a_ref[...].astype(F32) + other.astype(F32)).astype(BF16)


def settle_kernel(heads, keep_ref, got_ref, total_ref, gain_ref):
    total_ref[...] = keep_ref[...] + got_ref[...]
    gain_ref[...] = total_ref[heads : heads + 1, :]


def pair_kernel(a_ref, b_ref, o_ref):
    o_ref[...] = a_ref[...] + b_ref[...]


def spread_kernel(heads, total_ref, a_ref, b_ref, *outs):
    gain = a_ref[...] + b_ref[...]
    for s, out in enumerate(outs):
        rows = total_ref[8 * s : 8 * s + 8, :]
        out[...] = jnp.where(iota(rows.shape, 0) == heads, gain, rows)


def finish_kernel(at, k_ref, gain_ref, *refs):
    piece_refs = refs[:-2]
    kgrad_ref, vgrad_ref = refs[-2:]
    dim = k_ref.shape[1]
    rows = k_ref.shape[0]
    total = piece_refs[0][...].astype(F32) + piece_refs[1][at * rows :, :].astype(F32)
    for ref in piece_refs[2:]:
        total = total + ref[...].astype(F32)
    vgrad_ref[...] = total[dim:].T.astype(BF16)
    x = k_ref[...].astype(F32)
    rstd = rms(x)
    hat = x * rstd
    back = total[:dim].T * gain_ref[...]
    mean = jnp.mean(back * hat, axis=-1, keepdims=True)
    kgrad_ref[...] = (rstd * (back - hat * mean)).astype(BF16)


def forget_kernel(logit_ref, *refs):
    small_refs = refs[:-2]
    fgrad_ref, gains_ref = refs[-2:]
    heads = logit_ref.shape[0]
    small = small_refs[0][...]
    for ref in small_refs[1:]:
        small = small + ref[...]
    logit = logit_ref[...].astype(F32)
    fgrad_ref[...] = small[:heads] * (1.0 / (1.0 + jnp.exp(logit)))
    row = small[heads : heads + 1]
    dim = row.shape[1] // 2
    gains_ref[...] = jnp.concatenate([row[:, :dim], row[:, dim:]], axis=0)


def whole_step(queries, key_vectors, values, forget_logit, out_grad, query_gain, key_gain, lengths):
    n = lax.axis_size("seq")
    half = n // 2
    rows, full = queries.shape[1:]
    dim = query_gain.shape[0]
    heads = full // dim
    wide = heads * rows
    width = 2 * dim
    tall = dim + ONES
    query, grad, key, logit = queries[0], out_grad[0], key_vectors[0], forget_logit[0]
    qgain, kgain = query_gain[None], key_gain[None]
    matmul = 2 * rows * wide * width
    head_row = struct(heads, rows, dtype=F32)
    line = struct(1, wide, dtype=F32)
    state = struct(tall, wide, dtype=F32)
    key_sum = struct(dim, rows, dtype=F32)
    piece = struct(rows, width)
    wide_scratch = pltpu.VMEM((2, rows, wide), BF16)

    inputs = [lengths, key, values[0], logit, kgain]
    own, share, own_tail, low = kernel_call(
        pack_kernel, inputs,
        (
            struct(rows + TAIL, width), struct(TAIL, rows), struct(TAIL, rows),
            struct(8, 128, dtype=jnp.int32),
        ),
        near(inputs), far=5,
    )
    gather_order = [2] + list(range(n - 2, 2, -2))
    last = gather_order[-1] + 1
    blocks = {0: own}
    for k in gather_order:
        blocks[k] = swap(own, "seq", k)
    blocks[1] = swap(own, "seq", 1)
    share = swap(share, "seq", last)
    for k in gather_order:
        blocks[k + 1] = swap(blocks[k], "seq", 1)

    inputs = [lengths, query, grad, qgain]
    kaug_scratch = pltpu.VMEM((rows, width), BF16)
    qt, gt, acc, w0, kt0, extra = kernel_call(
        functools.partial(own_kernel, n), inputs + [own, own_tail],
        (
            struct(width, wide), struct(dim, wide), state, struct(rows, wide), struct(tall, rows),
            struct(n, TAIL, rows),
        ),
        [kaug_scratch] + near(inputs),
        flops=2 * matmul, far=4,
    )

    def stores(count):
        return struct(count, rows, wide), struct(count, tall, rows)

    ks_a = [1] + gather_order[:-1]
    ks_b = [gather_order[-1]] + [k + 1 for k in gather_order[:-1]]
    w_a, o_a, kt_a = kernel_call(
        functools.partial(early_kernel, ks_a),
        [low, qt, extra] + [blocks[k] for k in ks_a],
        (stores(half)[0], struct(half, tall, wide, dtype=F32), stores(half)[1]),
        [kaug_scratch],
        flops=2 * half * matmul,
    )
    w_b, acc, kt_b, between = kernel_call(
        functools.partial(second_kernel, n, heads, ks_a, ks_b, last),
        [low, qt, extra, acc, o_a, share] + [blocks[k] for k in range(1, n) if k != last],
        (stores(half - 1)[0], state, stores(half - 1)[1], struct(n, 1, wide, dtype=F32)),
        [kaug_scratch],
        flops=2 * half * matmul,
    )
    down = list(range(n - 1, 0, -2))
    odds = [down[: half // 2], down[half // 2 :]]
    kept = [w_a, kt_a, w_b, kt_b]
    results = kernel_call(
        functools.partial(middle_kernel, ks_a, ks_b, last, odds[0], heads),
        [low, qt, gt, extra, acc, between] + kept + [blocks[k] for k in [last] + odds[0]],
        (
            struct(dim, wide), state, line, line, key_sum, struct(rows, wide), struct(tall, rows),
            struct(len(odds[0]), 8, rows, dtype=F32), struct(len(odds[0]) * rows, width),
        ),
        [kaug_scratch, wide_scratch, wide_scratch],
        flops=4 * half * matmul,
    )
    mixed_t, acc, log_total, inner, key_acc, w_last, kt_last, gate_one, stack = results
    stacks = [swap(stack, "seq", 1)]
    results = kernel_call(
        functools.partial(middle_two_kernel, ks_a, ks_b, last, odds[1], heads),
        [low, qt, gt, acc, between, log_total, inner, key_acc] + kept + [w_last, kt_last]
        + [blocks[k] for k in odds[1]],
        (
            state, key_sum, struct(len(odds[1]), 8, rows, dtype=F32),
            struct(len(odds[1]) * rows, width),
        ),
        [wide_scratch, wide_scratch],
        flops=2 * half * matmul,
    )
    acc, key_acc, gate_two, stack = results
    stacks.append(swap(stack, "seq", 1))
    place = {k: (g, i) for g, ks in enumerate(odds) for i, k in enumerate(ks)}

    small = struct(8 * half, rows, dtype=F32)
    results = kernel_call(
        functools.partial(late_kernel, n, ks_a, ks_b, odds),
        [low, kgain, qgain, qt, gt, acc, between, log_total, inner, key_acc]
        + kept + [w0, kt0, gate_one, gate_two]
        + [blocks[2 * s] for s in range(half)],
        (state, small, small) + (piece,) * half,
        [pltpu.VMEM((dim, rows), F32), wide_scratch, wide_scratch, pltpu.VMEM((n, 8, rows), F32)],
        flops=4 * half * matmul,
    )
    acc, keep, give = results[:3]
    even = results[3:]

    got = swap(give, "seq", 1)
    query_grad, attention = kernel_call(
        query_kernel, [query, qgain, acc, mixed_t],
        (struct(rows, full), struct(rows, full)), flops=matmul,
    )
    arrived = [even[0], stacks[1]]
    for s in range(half - 1, 0, -1):
        group, at = place[2 * s + 1]
        both = kernel_call(functools.partial(add_kernel, at), [even[s], stacks[group]], piece)
        arrived.append(swap(both, "seq", 2 * s))
    eight = struct(8, rows, dtype=F32)
    gain_line = struct(1, width, dtype=F32)
    total, gain = kernel_call(
        functools.partial(settle_kernel, heads), [keep, got], (small, gain_line)
    )
    bit = 1
    while 2 * bit < lax.axis_size("rep"):
        gain = kernel_call(pair_kernel, [gain, swap(gain, "rep", bit)], gain_line)
        bit *= 2
    smalls = kernel_call(
        functools.partial(spread_kernel, heads),
        [total, gain, swap(gain, "rep", bit)], (eight,) * half,
    )
    smalls = [smalls[0]] + [swap(smalls[s], "seq", 2 * s) for s in range(1, half)]
    forget_grad, gains = kernel_call(
        forget_kernel, [logit] + smalls, (head_row, struct(2, dim, dtype=F32))
    )
    key_grad, value_grad = kernel_call(
        functools.partial(finish_kernel, place[1][1]), [key, kgain] + arrived, (struct(rows, dim), struct(rows, dim)),
        flops=matmul,
    )
    return (
        attention[None],
        query_grad[None],
        key_grad[None],
        value_grad[None],
        forget_grad[None],
        gains,
    )


def solution(mesh):
    return jax.shard_map(
        whole_step,
        mesh=mesh,
        in_specs=(
            P("rep", "seq", None),
            P("rep", "seq", None),
            P("rep", "seq", None),
            P("rep", None, "seq"),
            P("rep", "seq", None),
            P(),
            P(),
            P("rep", None),
        ),
        out_specs=(
            P("rep", "seq", None),
            P("rep", "seq", None),
            P("rep", "seq", None),
            P("rep", "seq", None),
            P("rep", None, "seq"),
            P(),
        ),
        check_vma=False,
    )
```
